32 devices in a mesh: dp: 16 (over z, y, core), ctx: 2 (over x).
Axes of the slice: x: 2, y: 2, z: 4, core: 2. Of those that a mesh axis runs over, the one named last changes fastest.
Arguments:
- tokens_in: bfloat16 [32, 512, 768], P('dp', 'ctx'), may hold values from -6 to 6
- live_mask: int32 [32], P('dp'), may hold values from 0 to 1, as said below
- cotangent: bfloat16 [32, 512, 768], P('dp', 'ctx'), may hold values from -6 to 6
- gains: bfloat16 [2, 768], P(None, ('dp', 'ctx')), may hold values from 0.099609375 to 1.8984375
- biases: bfloat16 [6, 768], P(None, ('dp', 'ctx')), may hold values from -3 to 3
- fc_bias: bfloat16 [3072], P(('dp', 'ctx')), may hold values from -3 to 3
- w_qkv: bfloat16 [768, 2304], P(('dp', 'ctx')), may hold values from -0.21875 to 0.21875
- w_out: bfloat16 [768, 768], P(('dp', 'ctx')), may hold values from -0.875 to 0.875
- w_fc: bfloat16 [768, 3072], P(('dp', 'ctx')), may hold values from -0.21875 to 0.21875
- w_proj: bfloat16 [3072, 768], P(('dp', 'ctx')), may hold values from -0.109375 to 0.109375
Outputs:
- block_out: bfloat16 [32, 512, 768], P('dp', 'ctx')
- grad_input: float32 [32, 512, 768], P('dp', 'ctx')
- grad_gains: float32 [2, 768], P(None, ('dp', 'ctx'))
- grad_biases: float32 [6, 768], P(None, ('dp', 'ctx'))
- grad_fc_bias: float32 [3072], P(('dp', 'ctx'))
- grad_w_qkv: float32 [768, 2304], P(('dp', 'ctx'))
- grad_w_out: float32 [768, 768], P(('dp', 'ctx'))
- grad_w_fc: float32 [768, 3072], P(('dp', 'ctx'))
- grad_w_proj: float32 [3072, 768], P(('dp', 'ctx'))
The draws below stay inside these ranges and needn't reach their ends.
Inputs may be any that keep to these rules, and one draw needn't show every extreme that they name: `live_mask`: the first of each data group's 2 slots always holds a sequence; some groups hold 2 sequences and some fewer in every draw.
All inputs are finite; a program needn't handle non-finite values.
Results may differ from the reference program's by a relative error of at most 0.012.
Values may be sent and summed in bfloat16 or wider, within the bound.
No kernel may reach another device: no remote copies, remote signals or barrier semaphores. Data moves between devices by JAX's collectives and lax.ppermute only.
A program may use at most 192 MiB of HBM per device.

```python
import jax
import jax.numpy as jnp
from jax import lax

D = 768
H = 12
HD = 64
FF = 3072
SEQ = 512
SLOTS = 2
SEQS = 32


def draw_live_mask(key, part):
    groups = SEQS // SLOTS
    flags = jax.random.randint(key, (groups, SLOTS), 0, 2)
    first = jnp.arange(SLOTS)[None, :] == 0
    flags = jnp.where(first, 1, flags)
    chosen = jax.random.randint(jax.random.fold_in(key, 7), (), 0, groups)
    group_ids = jnp.arange(groups)[:, None]
    flags = jnp.where(group_ids == chosen, 1, flags)
    flags = jnp.where((group_ids == (chosen + 1) % groups) & jnp.logical_not(first), 0, flags)
    return flags.reshape(SEQS).astype(jnp.int32)


def strengthened(result, key, source, target, parts, factor):
    def block_of(dim):
        return (jnp.arange(result.shape[dim]) // (result.shape[dim] // parts)).reshape((-1,) + (1,) * (result.ndim - 1 - dim))

    first = jax.random.permutation(key, parts)[block_of(target)]
    second = (block_of(target) + parts // 2) % parts
    return jnp.where((block_of(source) == first) | (block_of(source) == second), factor * result, result)


def levels(rng, extent, shards, low, high):
    factor_of = 1.0
    for axis_at, parts in shards:
        steps = jax.random.uniform(jax.random.fold_in(jax.random.fold_in(rng, 6), axis_at), (parts,), jnp.float32, low / len(shards), high / len(shards))
        factor_of = factor_of * jnp.repeat(jnp.exp(steps), extent[axis_at] // parts).reshape((-1,) + (1,) * (len(extent) - 1 - axis_at))
    return factor_of


def scatter_about(stream_key, extent, width, most, cuts=(), held_as=jnp.bfloat16):
    result = width * jax.random.normal(stream_key, extent, jnp.float32)
    if cuts:
        result = result * levels(stream_key, extent, cuts, -0.22, 0.18)
    return jnp.clip(result, -most, most).astype(held_as)


def gaussian_with(key, shape, width, bound, split, heavy, kind=jnp.bfloat16):
    result = width * jax.random.normal(key, shape, jnp.float32)
    if split:
        result = result * levels(key, shape, split, -0.22, 0.18)
    return jnp.clip(strengthened(result, jax.random.fold_in(key, 3), *heavy), -bound, bound).astype(kind)


def setup_inputs(seed: int = 0) -> dict:
    streams_of = jax.random.split(jax.random.key(seed), 11)
    tokens_in = scatter_about(streams_of[0], (SEQS, SEQ, D), 1.0, 6.0, ((0, 16), (1, 2)))
    live_mask = draw_live_mask(jax.random.fold_in(streams_of[10], 71), 0)
    cotangent = gaussian_with(streams_of[2], (SEQS, SEQ, D), 1.0, 6.0, ((0, 16), (1, 2)), (0, 2, 16, 2.0))
    gains = jnp.clip(1.0 + 0.18 * jax.random.normal(streams_of[3], (2, D), jnp.float32), 0.099609375, 1.8984375).astype(jnp.bfloat16)
    biases = scatter_about(streams_of[4], (6, D), 0.5, 3.0, ((1, 32),))
    fc_bias = scatter_about(streams_of[5], (FF,), 0.5, 3.0, ((0, 32),))
    w_qkv = scatter_about(streams_of[6], (D, 3 * D), D ** -0.5, 0.21875, ((0, 32),))
    w_out = scatter_about(streams_of[7], (D, D), (D // 16) ** -0.5, 0.875, ((0, 32),))
    w_fc = scatter_about(streams_of[8], (D, FF), D ** -0.5, 0.21875, ((0, 32),))
    w_proj = scatter_about(streams_of[9], (FF, D), FF ** -0.5, 0.109375, ((0, 32),))
    return dict(tokens_in=tokens_in, live_mask=live_mask, cotangent=cotangent, gains=gains, biases=biases, fc_bias=fc_bias, w_qkv=w_qkv, w_out=w_out, w_fc=w_fc, w_proj=w_proj)


NORM_EPS = 1e-05
SCORE_SCALE = 0.125
MASK_FILL = -1e+30

def layer_norm(values_in, gain, shift):
    center = values_in - lax.optimization_barrier(jnp.mean(values_in, -1, keepdims=True))
    inv_std = lax.rsqrt(lax.optimization_barrier(jnp.mean(center * center, -1, keepdims=True)) + NORM_EPS)
    normed = center * inv_std
    return (normed * gain + shift, normed, inv_std)

def norm_back(upstream, gain, normed, inv_std):
    scaled = upstream * gain
    return inv_std * (scaled - lax.optimization_barrier(jnp.mean(scaled, -1, keepdims=True)) - normed * lax.optimization_barrier(jnp.mean(scaled * normed, -1, keepdims=True)))

def gelu_back(pre_act, upstream):
    return jax.vjp(lambda values_in: jax.nn.gelu(values_in, approximate=True), pre_act)[1](upstream)[0]

def widen(narrow):
    return lax.optimization_barrier(narrow).astype(jnp.float32)

def reference(tokens_in, live_mask, cotangent, gains, biases, fc_bias, w_qkv, w_out, w_fc, w_proj):
    gain_rows = gains.astype(jnp.float32)
    bias_rows = biases.astype(jnp.float32)
    fc_shift = fc_bias.astype(jnp.float32)
    places = jnp.arange(SEQ)
    causal = places[None, :] <= places[:, None]

    def one_sequence(totals, inputs):
        seq_in, seq_cot, flag = inputs
        keep = flag.astype(jnp.float32)
        hidden_in = seq_in.astype(jnp.float32)
        ln_one, normed_one, inv_one = layer_norm(hidden_in, gain_rows[0], bias_rows[0])
        ln_one_b = ln_one.astype(jnp.bfloat16)
        projected = jnp.dot(ln_one_b, w_qkv, preferred_element_type=jnp.float32)
        queries = (projected[:, :D] + bias_rows[1]).astype(jnp.bfloat16)
        keys_all = projected[:, D:2 * D].astype(jnp.bfloat16)
        values_all = (projected[:, 2 * D:] + bias_rows[2]).astype(jnp.bfloat16)
        query_heads = widen(queries).reshape(SEQ, H, HD)
        key_heads = widen(keys_all).reshape(SEQ, H, HD)
        value_heads = widen(values_all).reshape(SEQ, H, HD)
        scores = jnp.einsum('qhd,khd->hqk', query_heads, key_heads) * SCORE_SCALE
        scores = jnp.where(causal[None], scores, MASK_FILL)
        peak = lax.optimization_barrier(jnp.max(scores, -1, keepdims=True))
        log_total = peak + jnp.log(lax.optimization_barrier(jnp.sum(jnp.exp(scores - peak), -1, keepdims=True)))
        probs = jnp.exp(scores - log_total)
        probs_wide = widen(probs.astype(jnp.bfloat16))
        attended = jnp.einsum('hqk,khd->qhd', probs_wide, value_heads).reshape(SEQ, D).astype(jnp.bfloat16)
        after_attn = hidden_in + jnp.dot(attended, w_out, preferred_element_type=jnp.float32) + bias_rows[3]
        ln_two, normed_two, inv_two = layer_norm(after_attn, gain_rows[1], bias_rows[4])
        ln_two_b = ln_two.astype(jnp.bfloat16)
        pre_act = jnp.dot(ln_two_b, w_fc, preferred_element_type=jnp.float32) + fc_shift
        activated = jax.nn.gelu(pre_act, approximate=True).astype(jnp.bfloat16)
        final = after_attn + jnp.dot(activated, w_proj, preferred_element_type=jnp.float32) + bias_rows[5]
        out_seq = (keep * final).astype(jnp.bfloat16)
        upstream = keep * seq_cot.astype(jnp.float32)
        upstream_b = upstream.astype(jnp.bfloat16)
        grad_proj = jnp.dot(activated.T, upstream_b, preferred_element_type=jnp.float32)
        d_act = jnp.dot(upstream_b, w_proj.T, preferred_element_type=jnp.float32)
        d_pre = gelu_back(pre_act, d_act)
        d_pre_b = d_pre.astype(jnp.bfloat16)
        grad_fc = jnp.dot(ln_two_b.T, d_pre_b, preferred_element_type=jnp.float32)
        d_ln_two = jnp.dot(d_pre_b, w_fc.T, preferred_element_type=jnp.float32)
        d_resid = upstream + norm_back(d_ln_two, gain_rows[1], normed_two, inv_two)
        d_resid_b = d_resid.astype(jnp.bfloat16)
        grad_out = jnp.dot(attended.T, d_resid_b, preferred_element_type=jnp.float32)
        d_att_b = jnp.dot(d_resid_b, w_out.T, preferred_element_type=jnp.float32).astype(jnp.bfloat16)
        d_att_heads = widen(d_att_b).reshape(SEQ, H, HD)
        att_heads = widen(attended).reshape(SEQ, H, HD)
        delta = jnp.einsum('qhd,qhd->hq', d_att_heads, att_heads)
        d_values = jnp.einsum('hqk,qhd->khd', probs_wide, d_att_heads).reshape(SEQ, D)
        d_probs = jnp.einsum('qhd,khd->hqk', d_att_heads, value_heads)
        d_scores = widen((probs * (d_probs - delta[:, :, None]) * SCORE_SCALE).astype(jnp.bfloat16))
        d_queries = jnp.einsum('hqk,khd->qhd', d_scores, key_heads).reshape(SEQ, D)
        d_keys = jnp.einsum('hqk,qhd->khd', d_scores, query_heads).reshape(SEQ, D)
        d_proj_in = jnp.concatenate([d_queries, d_keys, d_values], 1).astype(jnp.bfloat16)
        grad_qkv = jnp.dot(ln_one_b.T, d_proj_in, preferred_element_type=jnp.float32)
        d_ln_one = jnp.dot(d_proj_in, w_qkv.T, preferred_element_type=jnp.float32)
        d_input = d_resid + norm_back(d_ln_one, gain_rows[0], normed_one, inv_one)
        grad_gain = jnp.stack([lax.optimization_barrier(jnp.sum(d_ln_one * normed_one, 0)), lax.optimization_barrier(jnp.sum(d_ln_two * normed_two, 0))])
        grad_bias = jnp.stack([lax.optimization_barrier(jnp.sum(d_ln_one, 0)), lax.optimization_barrier(jnp.sum(d_queries, 0)), lax.optimization_barrier(jnp.sum(d_values, 0)), lax.optimization_barrier(jnp.sum(d_resid, 0)), lax.optimization_barrier(jnp.sum(d_ln_two, 0)), lax.optimization_barrier(jnp.sum(upstream, 0))])
        grad_shift = lax.optimization_barrier(jnp.sum(d_pre, 0))
        pieces = (grad_gain, grad_bias, grad_shift, grad_qkv, grad_out, grad_fc, grad_proj)
        return (jax.tree.map(jnp.add, totals, pieces), (out_seq, d_input))
    start = (jnp.zeros((2, D), jnp.float32), jnp.zeros((6, D), jnp.float32), jnp.zeros((FF,), jnp.float32), jnp.zeros((D, 3 * D), jnp.float32), jnp.zeros((D, D), jnp.float32), jnp.zeros((D, FF), jnp.float32), jnp.zeros((FF, D), jnp.float32))
    totals, (outputs, input_grads) = lax.scan(one_sequence, start, (tokens_in, cotangent, live_mask))
    return (outputs, input_grads, totals[0], totals[1], totals[2], totals[3], totals[4], totals[5], totals[6])
```

```python
import jax
import jax.numpy as jnp
from jax import lax
from jax.sharding import PartitionSpec as P

HD = 64
NORM_EPS = 1e-05
SCORE_SCALE = 0.125
MASK_FILL = -1e30
SMALL = 12
PAD = 128
BOTH = ("dp", "ctx")


def layer_norm(values_in, gain, shift):
    center = values_in - jnp.mean(values_in, -1, keepdims=True)
    inv_std = lax.rsqrt(jnp.mean(center * center, -1, keepdims=True) + NORM_EPS)
    normed = center * inv_std
    return (normed * gain + shift, normed, inv_std)


def norm_back(upstream, gain, normed, inv_std):
    scaled = upstream * gain
    return inv_std * (
        scaled
        - jnp.mean(scaled, -1, keepdims=True)
        - normed * jnp.mean(scaled * normed, -1, keepdims=True)
    )


def gelu_back(pre_act, upstream):
    return jax.vjp(lambda values_in: jax.nn.gelu(values_in, approximate=True), pre_act)[1](
        upstream
    )[0]


def rows_product(left, right):
    return lax.dot_general(
        left, right, (((0,), (0,)), ((), ())), preferred_element_type=jnp.float32
    )


def times_transposed(left, right):
    return lax.dot_general(
        left, right, (((1,), (1,)), ((), ())), preferred_element_type=jnp.float32
    )


GRID = (4, 2, 2, 2)


def on_grid():
    return lax.axis_size("dp") == 16 and lax.axis_size("ctx") == 2


def place():
    at = lax.axis_index("dp")
    return at // 4, (at // 2) % 2, at % 2, lax.axis_index("ctx")


def move(block, axis, step):
    pairs = []
    for source in range(32):
        spot = [source // 8, (source // 4) % 2, (source // 2) % 2, source % 2]
        spot[axis] = (spot[axis] + step) % GRID[axis]
        pairs.append((source, ((spot[0] * 2 + spot[1]) * 2 + spot[2]) * 2 + spot[3]))
    return lax.ppermute(block, BOTH, pairs)


def joined(mine, theirs, at, axis):
    first = at == 0
    return jnp.stack([jnp.where(first, mine, theirs), jnp.where(first, theirs, mine)], axis)


def cut_of(columns):
    return columns // 256 * 128


def gather(shard):
    if not on_grid():
        return lax.all_gather(shard, BOTH, axis=0, tiled=False)
    z, y, c, x = place()
    held = [shard] + [move(shard, 0, step) for step in (1, 2, 3)]
    rows = []
    for spot in range(4):
        source = (z - spot) % 4
        row = held[0]
        for step in (1, 2, 3):
            row = jnp.where(source == step, held[step], row)
        rows.append(row)
    ring = jnp.stack(rows, 0)
    cut = cut_of(shard.shape[1])
    left, right = ring[..., :cut], ring[..., cut:]
    left = joined(left, move(left, 1, 1), y, 1)
    right = joined(right, move(right, 3, 1), x, 1)
    left = joined(left, move(left, 3, 1), x, 2)
    right = joined(right, move(right, 1, 1), y, 1)
    half = jnp.concatenate([left, right], -1)
    return joined(half, move(half, 2, 1), c, 2)


def taken(block, at, axis):
    return lax.dynamic_index_in_dim(block, at, axis, keepdims=False)


def added(block, at, axis, arrived):
    total = taken(block, at, axis).astype(jnp.float32) + arrived.astype(jnp.float32)
    return total.astype(jnp.bfloat16)


def scatter(grads):
    devices = lax.axis_size("dp") * lax.axis_size("ctx")
    count, columns = grads.shape[0] // devices, grads.shape[1]
    if not on_grid():
        return lax.psum_scatter(
            grads.reshape(devices, count, columns), BOTH, scatter_dimension=0, tiled=False
        ).astype(jnp.float32)
    z, y, c, x = place()
    block = grads.reshape(GRID + (count, columns))
    half = added(block, c, 2, move(taken(block, 1 - c, 2), 2, 1))
    cut = cut_of(columns)
    left, right = half[..., :cut], half[..., cut:]
    left = added(left, x, 2, move(taken(left, 1 - x, 2), 3, 1))
    right = added(right, y, 1, move(taken(right, 1 - y, 1), 1, 1))
    left = added(left, y, 1, move(taken(left, 1 - y, 1), 1, 1))
    right = added(right, x, 1, move(taken(right, 1 - x, 1), 3, 1))
    ring = jnp.concatenate([left, right], -1)
    total = taken(ring, z, 0).astype(jnp.float32)
    for step in (1, 2, 3):
        total = total + move(taken(ring, (z + step) % 4, 0), 0, step).astype(jnp.float32)
    return total


def on_device(tokens_in, live_mask, cotangent, gains, biases, fc_bias, w_qkv, w_out, w_fc, w_proj):
    slot_count, span, width = tokens_in.shape
    row_count = slot_count * span
    head_count = width // HD
    devices = lax.axis_size("dp") * lax.axis_size("ctx")
    own_cols = width // devices
    units = fc_bias.shape[0] * devices
    per_col = units // width
    paired = lax.axis_size("ctx") == 2

    small = jnp.concatenate([gains.T, biases.T, fc_bias.reshape(own_cols, per_col)], 1)
    small = jnp.pad(small, ((0, 0), (0, PAD - SMALL)))
    first = gather(jnp.concatenate([w_qkv, small], 1)).reshape(width, 3 * width + PAD)
    rest = lax.all_gather(
        jnp.concatenate(
            [w_out] + [w_fc[:, i * width : (i + 1) * width] for i in range(per_col)] + [w_proj], 0
        ),
        BOTH,
        axis=0,
        tiled=False,
    )
    qkv_weight = first[:, : 3 * width]
    small_all = first[:, 3 * width : 3 * width + SMALL].astype(jnp.float32)
    gain_rows = small_all[:, :2].T
    bias_rows = small_all[:, 2:8].T
    fc_shift = small_all[:, 8:].reshape(units)
    out_weight = rest[:, :own_cols].reshape(width, width)
    fc_weight = jnp.concatenate(
        [
            rest[:, (i + 1) * own_cols : (i + 2) * own_cols].reshape(width, width)
            for i in range(per_col)
        ],
        1,
    )
    proj_weight = rest[:, (1 + per_col) * own_cols :].reshape(units, width)

    keep_rows = jnp.repeat(live_mask.astype(jnp.float32), span)[:, None]
    hidden_in = tokens_in.reshape(row_count, width).astype(jnp.float32)
    ln_one, normed_one, inv_one = layer_norm(hidden_in, gain_rows[0], bias_rows[0])
    ln_one_b = ln_one.astype(jnp.bfloat16)
    projected = jnp.dot(ln_one_b, qkv_weight, preferred_element_type=jnp.float32)
    queries = (projected[:, :width] + bias_rows[1]).astype(jnp.bfloat16)
    keys_local = projected[:, width : 2 * width].astype(jnp.bfloat16)
    values_local = (projected[:, 2 * width :] + bias_rows[2]).astype(jnp.bfloat16)
    key_value = jnp.concatenate([keys_local, values_local], 1).reshape(slot_count, span, 2 * width)
    rank = lax.axis_index("ctx")
    if paired:
        pairs = [(2 * i, 2 * i + 1) for i in range(devices // 2)]
        before = lax.ppermute(key_value, BOTH, pairs)
        kv_whole = jnp.concatenate([before, key_value], 1)
        seq_len = 2 * span
        row_at, col_at = jnp.arange(span)[:, None], jnp.arange(seq_len)[None, :]
        causal = jnp.where(col_at < span, rank == 1, col_at - span <= row_at)
    else:
        kv_whole = lax.all_gather(key_value, "ctx", axis=1, tiled=True)
        seq_len = kv_whole.shape[1]
        query_place = rank * span + jnp.arange(span)
        causal = jnp.arange(seq_len)[None, :] <= query_place[:, None]
    query_heads = queries.reshape(slot_count, span, head_count, HD)
    key_heads = kv_whole[:, :, :width].reshape(slot_count, seq_len, head_count, HD)
    value_heads = kv_whole[:, :, width:].reshape(slot_count, seq_len, head_count, HD)

    def score_block(slot_id):
        scores = (
            jnp.einsum(
                "qhd,khd->hqk",
                query_heads[slot_id],
                key_heads[slot_id],
                preferred_element_type=jnp.float32,
            )
            * SCORE_SCALE
        )
        return jnp.where(causal[None], scores, MASK_FILL)

    log_totals = []
    attended_list = []
    for slot_id in range(slot_count):
        scores = score_block(slot_id)
        peak = jnp.max(scores, -1, keepdims=True)
        log_total = peak + jnp.log(jnp.sum(jnp.exp(scores - peak), -1, keepdims=True))
        probs_b = jnp.exp(scores - log_total).astype(jnp.bfloat16)
        attended_list.append(
            jnp.einsum(
                "hqk,khd->qhd", probs_b, value_heads[slot_id], preferred_element_type=jnp.float32
            )
            .reshape(span, width)
            .astype(jnp.bfloat16)
        )
        log_totals.append(log_total)
    attended = jnp.concatenate(attended_list, 0)
    after_attn = (
        hidden_in + jnp.dot(attended, out_weight, preferred_element_type=jnp.float32) + bias_rows[3]
    )
    ln_two, normed_two, inv_two = layer_norm(after_attn, gain_rows[1], bias_rows[4])
    ln_two_b = ln_two.astype(jnp.bfloat16)
    pre_act = jnp.dot(ln_two_b, fc_weight, preferred_element_type=jnp.float32) + fc_shift
    activated = jax.nn.gelu(pre_act, approximate=True).astype(jnp.bfloat16)
    final = (
        after_attn
        + jnp.dot(activated, proj_weight, preferred_element_type=jnp.float32)
        + bias_rows[5]
    )
    block_out = (keep_rows * final).astype(jnp.bfloat16).reshape(slot_count, span, width)

    upstream = keep_rows * cotangent.reshape(row_count, width).astype(jnp.float32)
    upstream_b = upstream.astype(jnp.bfloat16)
    out_proj = scatter(rows_product(activated, upstream_b).astype(jnp.bfloat16))
    d_act = times_transposed(upstream_b, proj_weight)
    d_pre = gelu_back(pre_act, d_act)
    d_pre_b = d_pre.astype(jnp.bfloat16)
    grad_fc = rows_product(ln_two_b, d_pre_b).astype(jnp.bfloat16)
    d_ln_two = times_transposed(d_pre_b, fc_weight)
    d_resid = upstream + norm_back(d_ln_two, gain_rows[1], normed_two, inv_two)
    d_resid_b = d_resid.astype(jnp.bfloat16)
    grad_out = rows_product(attended, d_resid_b).astype(jnp.bfloat16)
    middle = scatter(jnp.concatenate([grad_fc, grad_out], 1))
    out_fc, out_out = middle[:, :units], middle[:, units:]
    d_att_b = times_transposed(d_resid_b, out_weight).astype(jnp.bfloat16)
    d_att_heads = d_att_b.reshape(slot_count, span, head_count, HD)
    att_heads = attended.reshape(slot_count, span, head_count, HD)
    query_grads = []
    term_list = []
    for slot_id in range(slot_count):
        scores = score_block(slot_id)
        probs = jnp.exp(scores - log_totals[slot_id])
        delta = jnp.einsum(
            "qhd,qhd->hq",
            d_att_heads[slot_id],
            att_heads[slot_id],
            preferred_element_type=jnp.float32,
        )
        d_probs = jnp.einsum(
            "qhd,khd->hqk",
            d_att_heads[slot_id],
            value_heads[slot_id],
            preferred_element_type=jnp.float32,
        )
        d_scores = (probs * (d_probs - delta[:, :, None]) * SCORE_SCALE).astype(jnp.bfloat16)
        query_grads.append(
            jnp.einsum(
                "hqk,khd->qhd", d_scores, key_heads[slot_id], preferred_element_type=jnp.float32
            ).reshape(span, width)
        )
        probs_b = probs.astype(jnp.bfloat16)
        d_values = jnp.einsum(
            "hqk,qhd->khd", probs_b, d_att_heads[slot_id], preferred_element_type=jnp.float32
        )
        d_keys = jnp.einsum(
            "hqk,qhd->khd", d_scores, query_heads[slot_id], preferred_element_type=jnp.float32
        )
        term_list.append(
            jnp.concatenate([d_keys.reshape(seq_len, width), d_values.reshape(seq_len, width)], 1)
        )
    key_terms = jnp.stack(term_list)
    if paired:
        back = [(2 * i + 1, 2 * i) for i in range(devices // 2)]
        arrived = lax.ppermute(key_terms[:, :span].astype(jnp.bfloat16), BOTH, back)
        key_grads = key_terms[:, span:] + arrived.astype(jnp.float32)
    else:
        key_grads = lax.psum_scatter(
            key_terms.astype(jnp.bfloat16), "ctx", scatter_dimension=1, tiled=True
        ).astype(jnp.float32)
    key_grads = key_grads.reshape(row_count, 2 * width)
    d_queries = jnp.concatenate(query_grads, 0)
    d_values_own = key_grads[:, width:]
    d_proj_in = jnp.concatenate([d_queries, key_grads], 1).astype(jnp.bfloat16)
    grad_qkv = rows_product(ln_one_b, d_proj_in).astype(jnp.bfloat16)
    d_ln_one = times_transposed(d_proj_in, qkv_weight)
    d_input = d_resid + norm_back(d_ln_one, gain_rows[0], normed_one, inv_one)
    grad_small = jnp.stack(
        [
            jnp.sum(d_ln_one * normed_one, 0),
            jnp.sum(d_ln_two * normed_two, 0),
            jnp.sum(d_ln_one, 0),
            jnp.sum(d_queries, 0),
            jnp.sum(d_values_own, 0),
            jnp.sum(d_resid, 0),
            jnp.sum(d_ln_two, 0),
            jnp.sum(upstream, 0),
        ],
        1,
    )
    grad_shift = jnp.sum(d_pre, 0).reshape(width, per_col)
    grad_small = jnp.concatenate([grad_small, grad_shift], 1).astype(jnp.bfloat16)
    grad_small = jnp.pad(grad_small, ((0, 0), (0, PAD - SMALL)))
    last = scatter(jnp.concatenate([grad_qkv, grad_small], 1))
    out_qkv = last[:, : 3 * width]
    own = last[:, 3 * width : 3 * width + SMALL]
    return (
        block_out,
        d_input.reshape(slot_count, span, width),
        own[:, :2].T,
        own[:, 2:8].T,
        own[:, 8:].reshape(own_cols * per_col),
        out_qkv,
        out_out,
        out_fc,
        out_proj,
    )


def solution(mesh):
    in_specs = (
        P("dp", "ctx", None),
        P("dp"),
        P("dp", "ctx", None),
        P(None, ("dp", "ctx")),
        P(None, ("dp", "ctx")),
        P(("dp", "ctx")),
        P(("dp", "ctx"), None),
        P(("dp", "ctx"), None),
        P(("dp", "ctx"), None),
        P(("dp", "ctx"), None),
    )
    out_specs = (
        P("dp", "ctx", None),
        P("dp", "ctx", None),
        P(None, ("dp", "ctx")),
        P(None, ("dp", "ctx")),
        P(("dp", "ctx")),
        P(("dp", "ctx"), None),
        P(("dp", "ctx"), None),
        P(("dp", "ctx"), None),
        P(("dp", "ctx"), None),
    )
    return jax.shard_map(
        on_device, mesh=mesh, in_specs=in_specs, out_specs=out_specs, check_vma=False
    )
```

```python
import jax
import jax.numpy as jnp
from jax import lax
from jax.experimental import pallas as pl
from jax.experimental.pallas import tpu as pltpu
from jax.sharding import PartitionSpec as P

HD = 64
NORM_EPS = 1e-05
SCORE_SCALE = 0.125
MASK_FILL = -1e30
SMALL = 12
PAD = 128
BOTH = ("dp", "ctx")


def layer_norm(values_in, gain, shift):
    center = values_in - jnp.mean(values_in, -1, keepdims=True)
    inv_std = lax.rsqrt(jnp.mean(center * center, -1, keepdims=True) + NORM_EPS)
    normed = center * inv_std
    return (normed * gain + shift, normed, inv_std)


def norm_back(upstream, gain, normed, inv_std):
    scaled = upstream * gain
    return inv_std * (
        scaled
        - jnp.mean(scaled, -1, keepdims=True)
        - normed * jnp.mean(scaled * normed, -1, keepdims=True)
    )


def gelu_back(pre_act, upstream):
    return jax.vjp(lambda values_in: jax.nn.gelu(values_in, approximate=True), pre_act)[1](
        upstream
    )[0]


def rows_product(left, right):
    return lax.dot_general(
        left, right, (((0,), (0,)), ((), ())), preferred_element_type=jnp.float32
    )


def times_transposed(left, right):
    return lax.dot_general(
        left, right, (((1,), (1,)), ((), ())), preferred_element_type=jnp.float32
    )


GRID = (4, 2, 2, 2)


def on_grid():
    return lax.axis_size("dp") == 16 and lax.axis_size("ctx") == 2


def place():
    at = lax.axis_index("dp")
    return at // 4, (at // 2) % 2, at % 2, lax.axis_index("ctx")


def move(block, axis, step):
    pairs = []
    for source in range(32):
        spot = [source // 8, (source // 4) % 2, (source // 2) % 2, source % 2]
        spot[axis] = (spot[axis] + step) % GRID[axis]
        pairs.append((source, ((spot[0] * 2 + spot[1]) * 2 + spot[2]) * 2 + spot[3]))
    return lax.ppermute(block, BOTH, pairs)


def joined(mine, theirs, at, axis):
    first = at == 0
    return jnp.stack([jnp.where(first, mine, theirs), jnp.where(first, theirs, mine)], axis)


def cut_of(columns):
    return columns // 256 * 128


def gather(shard):
    if not on_grid():
        return lax.all_gather(shard, BOTH, axis=0, tiled=False)
    z, y, c, x = place()
    held = [shard] + [move(shard, 0, step) for step in (1, 2, 3)]
    rows = []
    for spot in range(4):
        source = (z - spot) % 4
        row = held[0]
        for step in (1, 2, 3):
            row = jnp.where(source == step, held[step], row)
        rows.append(row)
    ring = jnp.stack(rows, 0)
    cut = cut_of(shard.shape[1])
    left, right = ring[..., :cut], ring[..., cut:]
    left = joined(left, move(left, 1, 1), y, 1)
    right = joined(right, move(right, 3, 1), x, 1)
    left = joined(left, move(left, 3, 1), x, 2)
    right = joined(right, move(right, 1, 1), y, 1)
    half = jnp.concatenate([left, right], -1)
    return joined(half, move(half, 2, 1), c, 2)


def taken(block, at, axis):
    return lax.dynamic_index_in_dim(block, at, axis, keepdims=False)


def added(block, at, axis, arrived):
    total = taken(block, at, axis).astype(jnp.float32) + arrived.astype(jnp.float32)
    return total.astype(jnp.bfloat16)


class Scatter:
    def __init__(self, grads):
        devices = lax.axis_size("dp") * lax.axis_size("ctx")
        count, columns = grads.shape[0] // devices, grads.shape[1]
        self.grid = on_grid()
        self.cut = cut_of(columns)
        self.held = grads.reshape((GRID if self.grid else (devices,)) + (count, columns))

    def core(self):
        if self.grid:
            c = place()[2]
            half = added(self.held, c, 2, move(taken(self.held, 1 - c, 2), 2, 1))
            self.held = (half[..., : self.cut], half[..., self.cut :])

    def first(self):
        if self.grid:
            _, y, _, x = place()
            left, right = self.held
            left = added(left, x, 2, move(taken(left, 1 - x, 2), 3, 1))
            right = added(right, y, 1, move(taken(right, 1 - y, 1), 1, 1))
            self.held = (left, right)

    def second(self):
        if self.grid:
            _, y, _, x = place()
            left, right = self.held
            left = added(left, y, 1, move(taken(left, 1 - y, 1), 1, 1))
            right = added(right, x, 1, move(taken(right, 1 - x, 1), 3, 1))
            self.held = jnp.concatenate([left, right], -1)

    def last(self):
        if not self.grid:
            return lax.psum_scatter(self.held, BOTH, scatter_dimension=0, tiled=False).astype(
                jnp.float32
            )
        z = place()[0]
        total = taken(self.held, z, 0).astype(jnp.float32)
        for step in (1, 2, 3):
            sent = taken(self.held, (z + step) % 4, 0)
            total = total + move(sent, 0, step).astype(jnp.float32)
        return total

    def all(self):
        self.core()
        self.first()
        self.second()
        return self.last()


def gate(value, *scatters):
    value, held = lax.optimization_barrier((value, [each.held for each in scatters]))
    for each, now in zip(scatters, held):
        each.held = now
    return value


LANES = 128


def one_head(block, head):
    lane = lax.broadcasted_iota(jnp.int32, block.shape, 1)
    return jnp.where(lane // HD == head, block, jnp.zeros_like(block))


def by_rows(left, right):
    return lax.dot_general(
        left, right, (((1,), (1,)), ((), ())), preferred_element_type=jnp.float32
    )


def own_scores(keys, queries):
    scores = by_rows(keys, queries) * SCORE_SCALE
    key_at = lax.broadcasted_iota(jnp.int32, scores.shape, 0)
    query_at = lax.broadcasted_iota(jnp.int32, scores.shape, 1)
    return jnp.where(key_at <= query_at, scores, MASK_FILL)


def far_scores(keys, queries, limit):
    scores = by_rows(keys, queries) * SCORE_SCALE
    key_at = lax.broadcasted_iota(jnp.int32, scores.shape, 0)
    return jnp.where(key_at < limit, scores, MASK_FILL)


def transposed(block):
    return block.astype(jnp.float32).T


def attend_kernel(limit, q_ref, ko_ref, vo_ref, kf_ref, vf_ref, out_ref, log_ref):
    own_values = transposed(vo_ref[0]).astype(jnp.bfloat16)
    far_values = transposed(vf_ref[0]).astype(jnp.bfloat16)
    parts = []
    for head in range(LANES // HD):
        rows = slice(head * HD, (head + 1) * HD)
        queries = one_head(q_ref[0], head)
        own = own_scores(ko_ref[0], queries)
        far = far_scores(kf_ref[0], queries, limit[0])
        peak = jnp.maximum(jnp.max(own, 0, keepdims=True), jnp.max(far, 0, keepdims=True))
        own = jnp.exp(own - peak)
        far = jnp.exp(far - peak)
        total = jnp.sum(own, 0, keepdims=True) + jnp.sum(far, 0, keepdims=True)
        log_ref[0, 0, head : head + 1, :] = peak + jnp.log(total)
        scale = 1.0 / total
        own = (own * scale).astype(jnp.bfloat16)
        far = (far * scale).astype(jnp.bfloat16)
        parts.append(
            jnp.dot(own_values[rows], own, preferred_element_type=jnp.float32)
            + jnp.dot(far_values[rows], far, preferred_element_type=jnp.float32)
        )
    out_ref[0] = jnp.concatenate(parts, 0).T.astype(jnp.bfloat16)


def block_back(q, keys, values, d_att, attended, logs, scores_of):
    products = (d_att.astype(jnp.float32) * attended.astype(jnp.float32)).T
    keys_across = transposed(keys).astype(jnp.bfloat16)
    d_queries, d_keys, d_values = [], None, None
    for head in range(LANES // HD):
        rows = slice(head * HD, (head + 1) * HD)
        queries, d_head = one_head(q, head), one_head(d_att, head)
        delta = jnp.sum(products[rows], 0, keepdims=True)
        probs = jnp.exp(scores_of(keys, queries) - logs[head : head + 1])
        d_probs = by_rows(values, d_head)
        d_scores = (probs * (d_probs - delta) * SCORE_SCALE).astype(jnp.bfloat16)
        values_term = jnp.dot(
            probs.astype(jnp.bfloat16), d_head, preferred_element_type=jnp.float32
        )
        keys_term = jnp.dot(d_scores, queries, preferred_element_type=jnp.float32)
        d_values = values_term if head == 0 else d_values + values_term
        d_keys = keys_term if head == 0 else d_keys + keys_term
        d_queries.append(jnp.dot(keys_across[rows], d_scores, preferred_element_type=jnp.float32))
    return jnp.concatenate(d_queries, 0).T, d_keys, d_values


def far_kernel(limit, q_ref, k_ref, v_ref, d_ref, o_ref, log_ref, dq_ref, dkv_ref):
    d_queries, d_keys, d_values = block_back(
        q_ref[0], k_ref[0], v_ref[0], d_ref[0], o_ref[0], log_ref[0, 0],
        lambda keys, queries: far_scores(keys, queries, limit[0]),
    )
    dq_ref[0] = d_queries
    dkv_ref[0, 0] = d_keys.astype(jnp.bfloat16)
    dkv_ref[0, 1] = d_values.astype(jnp.bfloat16)


def own_kernel(
    q_ref, k_ref, v_ref, d_ref, o_ref, log_ref, before_ref, dq_ref, sum_ref, dkv_ref
):
    d_queries, d_keys, d_values = block_back(
        q_ref[0], k_ref[0], v_ref[0], d_ref[0], o_ref[0], log_ref[0, 0], own_scores
    )
    d_queries = d_queries + before_ref[0]
    dq_ref[0] = d_queries.astype(jnp.bfloat16)
    sum_ref[0] = jnp.sum(d_queries, 0, keepdims=True)
    dkv_ref[0, 0] = d_keys
    dkv_ref[0, 1] = d_values


def rows_spec(rows, skip=0):
    return pl.BlockSpec((1, rows, LANES), lambda s, p, *_: (s, 0, p + skip))


def log_spec(span):
    return pl.BlockSpec((1, 1, LANES // HD, span), lambda s, p, *_: (s, p, 0, 0))


def pair_spec(rows):
    return pl.BlockSpec((1, 2, rows, LANES), lambda s, p, *_: (s, 0, 0, p))


def attend(limit, queries, near, far):
    slots, span, width = queries.shape
    groups, reach = width // LANES, far.shape[1]
    return pl.pallas_call(
        attend_kernel,
        grid_spec=pltpu.PrefetchScalarGridSpec(
            num_scalar_prefetch=1,
            grid=(slots, groups),
            in_specs=[
                rows_spec(span),
                rows_spec(span),
                rows_spec(span, groups),
                rows_spec(reach),
                rows_spec(reach, groups),
            ],
            out_specs=[rows_spec(span), log_spec(span)],
        ),
        out_shape=[
            jax.ShapeDtypeStruct(queries.shape, jnp.bfloat16),
            jax.ShapeDtypeStruct((slots, groups, LANES // HD, span), jnp.float32),
        ],
        name="attend",
    )(limit, queries, near, near, far, far)


def far_back(limit, queries, far, d_att, attended, logs):
    slots, span, width = queries.shape
    groups, reach = width // LANES, far.shape[1]
    return pl.pallas_call(
        far_kernel,
        grid_spec=pltpu.PrefetchScalarGridSpec(
            num_scalar_prefetch=1,
            grid=(slots, groups),
            in_specs=[
                rows_spec(span),
                rows_spec(reach),
                rows_spec(reach, groups),
                rows_spec(span),
                rows_spec(span),
                log_spec(span),
            ],
            out_specs=[rows_spec(span), pair_spec(reach)],
        ),
        out_shape=[
            jax.ShapeDtypeStruct(queries.shape, jnp.float32),
            jax.ShapeDtypeStruct((slots, 2, reach, width), jnp.bfloat16),
        ],
        name="far_back",
    )(limit, queries, far, far, d_att, attended, logs)


def own_back(queries, near, d_att, attended, logs, before):
    slots, span, width = queries.shape
    groups = width // LANES
    return pl.pallas_call(
        own_kernel,
        grid=(slots, groups),
        in_specs=[
            rows_spec(span),
            rows_spec(span),
            rows_spec(span, groups),
            rows_spec(span),
            rows_spec(span),
            log_spec(span),
            rows_spec(span),
        ],
        out_specs=[
            rows_spec(span),
            pl.BlockSpec((1, 1, LANES), lambda s, p: (s, 0, p)),
            pair_spec(span),
        ],
        out_shape=[
            jax.ShapeDtypeStruct(queries.shape, jnp.bfloat16),
            jax.ShapeDtypeStruct((slots, 1, width), jnp.float32),
            jax.ShapeDtypeStruct((slots, 2, span, width), jnp.float32),
        ],
        name="own_back",
    )(queries, near, near, d_att, attended, logs, before)


def on_device(tokens_in, live_mask, cotangent, gains, biases, fc_bias, w_qkv, w_out, w_fc, w_proj):
    slot_count, span, width = tokens_in.shape
    row_count = slot_count * span
    devices = lax.axis_size("dp") * lax.axis_size("ctx")
    own_cols = width // devices
    units = fc_bias.shape[0] * devices
    per_col = units // width
    paired = lax.axis_size("ctx") == 2

    small = jnp.concatenate([gains.T, biases.T, fc_bias.reshape(own_cols, per_col)], 1)
    small = jnp.pad(small, ((0, 0), (0, PAD - SMALL)))
    first = gather(jnp.concatenate([w_qkv, small], 1)).reshape(width, 3 * width + PAD)
    rest = lax.all_gather(
        jnp.concatenate(
            [w_out] + [w_fc[:, i * width : (i + 1) * width] for i in range(per_col)] + [w_proj], 0
        ),
        BOTH,
        axis=0,
        tiled=False,
    )
    qkv_weight = first[:, : 3 * width]
    small_all = first[:, 3 * width : 3 * width + SMALL].astype(jnp.float32)
    gain_rows = small_all[:, :2].T
    bias_rows = small_all[:, 2:8].T
    fc_shift = small_all[:, 8:].reshape(units)
    out_weight = rest[:, :own_cols].reshape(width, width)
    fc_weight = jnp.concatenate(
        [
            rest[:, (i + 1) * own_cols : (i + 2) * own_cols].reshape(width, width)
            for i in range(per_col)
        ],
        1,
    )
    proj_weight = rest[:, (1 + per_col) * own_cols :].reshape(units, width)

    keep_rows = jnp.repeat(live_mask.astype(jnp.float32), span)[:, None]
    hidden_in = tokens_in.reshape(row_count, width).astype(jnp.float32)
    ln_one, normed_one, inv_one = layer_norm(hidden_in, gain_rows[0], bias_rows[0])
    ln_one_b = ln_one.astype(jnp.bfloat16)
    projected = jnp.dot(ln_one_b, qkv_weight, preferred_element_type=jnp.float32)
    queries = (projected[:, :width] + bias_rows[1]).astype(jnp.bfloat16)
    keys_local = projected[:, width : 2 * width].astype(jnp.bfloat16)
    values_local = (projected[:, 2 * width :] + bias_rows[2]).astype(jnp.bfloat16)
    key_value = jnp.concatenate([keys_local, values_local], 1).reshape(slot_count, span, 2 * width)
    rank = lax.axis_index("ctx")
    limit = (rank * span).reshape(1).astype(jnp.int32)
    if paired:
        pairs = [(2 * i, 2 * i + 1) for i in range(devices // 2)]
        before = lax.ppermute(key_value, BOTH, pairs)
    else:
        before = lax.all_gather(key_value, "ctx", axis=1, tiled=True)
    queries = queries.reshape(slot_count, span, width)
    attended3, logs = attend(limit, queries, key_value, before)
    attended = attended3.reshape(row_count, width)
    after_attn = (
        hidden_in + jnp.dot(attended, out_weight, preferred_element_type=jnp.float32) + bias_rows[3]
    )
    ln_two, normed_two, inv_two = layer_norm(after_attn, gain_rows[1], bias_rows[4])
    ln_two_b = ln_two.astype(jnp.bfloat16)
    pre_act = jnp.dot(ln_two_b, fc_weight, preferred_element_type=jnp.float32) + fc_shift
    activated = jax.nn.gelu(pre_act, approximate=True).astype(jnp.bfloat16)
    final = (
        after_attn
        + jnp.dot(activated, proj_weight, preferred_element_type=jnp.float32)
        + bias_rows[5]
    )
    block_out = (keep_rows * final).astype(jnp.bfloat16).reshape(slot_count, span, width)

    upstream = keep_rows * cotangent.reshape(row_count, width).astype(jnp.float32)
    upstream_b = upstream.astype(jnp.bfloat16)
    sum_proj = Scatter(rows_product(activated, upstream_b).astype(jnp.bfloat16))
    sum_proj.core()
    d_act = times_transposed(upstream_b, proj_weight)
    d_pre = gelu_back(pre_act, d_act)
    d_pre_b = gate(d_pre.astype(jnp.bfloat16), sum_proj)
    sum_proj.first()
    grad_fc = rows_product(ln_two_b, d_pre_b).astype(jnp.bfloat16)
    d_ln_two = times_transposed(d_pre_b, fc_weight)
    d_resid = upstream + norm_back(d_ln_two, gain_rows[1], normed_two, inv_two)
    d_resid_b = d_resid.astype(jnp.bfloat16)
    grad_out = rows_product(attended, d_resid_b).astype(jnp.bfloat16)
    sum_fc = Scatter(jnp.concatenate([grad_fc, grad_out], 1))
    d_att = times_transposed(d_resid_b, out_weight).astype(jnp.bfloat16)
    d_att = gate(d_att, sum_proj, sum_fc).reshape(slot_count, span, width)
    sum_fc.core()
    sum_proj.second()
    d_far, far_terms = far_back(limit, queries, before, d_att, attended3, logs)
    far_terms = gate(far_terms, sum_proj, sum_fc)
    if paired:
        back = [(2 * i + 1, 2 * i) for i in range(devices // 2)]
        arrived = lax.ppermute(far_terms, BOTH, back)
    else:
        arrived = lax.psum_scatter(far_terms, "ctx", scatter_dimension=2, tiled=True)
    sum_fc.first()
    out_proj = sum_proj.last()
    d_queries, query_sums, own_terms = own_back(
        queries, key_value, d_att, attended3, logs, gate(d_far, sum_proj)
    )
    d_queries = gate(d_queries, sum_fc)
    sum_fc.second()
    own_terms = own_terms + arrived.astype(jnp.float32)
    own_terms = gate(own_terms, sum_fc)
    middle = sum_fc.last()
    out_fc, out_out = middle[:, :units], middle[:, units:]
    d_keys = own_terms[:, 0].reshape(row_count, width)
    d_values_own = own_terms[:, 1].reshape(row_count, width)
    d_proj_in = jnp.concatenate(
        [
            d_queries.reshape(row_count, width),
            d_keys.astype(jnp.bfloat16),
            d_values_own.astype(jnp.bfloat16),
        ],
        1,
    )
    grad_qkv = rows_product(ln_one_b, d_proj_in).astype(jnp.bfloat16)
    d_ln_one = times_transposed(d_proj_in, qkv_weight)
    d_input = d_resid + norm_back(d_ln_one, gain_rows[0], normed_one, inv_one)
    grad_small = jnp.stack(
        [
            jnp.sum(d_ln_one * normed_one, 0),
            jnp.sum(d_ln_two * normed_two, 0),
            jnp.sum(d_ln_one, 0),
            jnp.sum(query_sums, (0, 1)),
            jnp.sum(d_values_own, 0),
            jnp.sum(d_resid, 0),
            jnp.sum(d_ln_two, 0),
            jnp.sum(upstream, 0),
        ],
        1,
    )
    grad_shift = jnp.sum(d_pre, 0).reshape(width, per_col)
    grad_small = jnp.concatenate([grad_small, grad_shift], 1).astype(jnp.bfloat16)
    grad_small = jnp.pad(grad_small, ((0, 0), (0, PAD - SMALL)))
    last = Scatter(jnp.concatenate([grad_qkv, grad_small], 1)).all()
    out_qkv = last[:, : 3 * width]
    own = last[:, 3 * width : 3 * width + SMALL]
    return (
        block_out,
        d_input.reshape(slot_count, span, width),
        own[:, :2].T,
        own[:, 2:8].T,
        own[:, 8:].reshape(own_cols * per_col),
        out_qkv,
        out_out,
        out_fc,
        out_proj,
    )


def solution(mesh):
    in_specs = (
        P("dp", "ctx", None),
        P("dp"),
        P("dp", "ctx", None),
        P(None, ("dp", "ctx")),
        P(None, ("dp", "ctx")),
        P(("dp", "ctx")),
        P(("dp", "ctx"), None),
        P(("dp", "ctx"), None),
        P(("dp", "ctx"), None),
        P(("dp", "ctx"), None),
    )
    out_specs = (
        P("dp", "ctx", None),
        P("dp", "ctx", None),
        P(None, ("dp", "ctx")),
        P(None, ("dp", "ctx")),
        P(("dp", "ctx")),
        P(("dp", "ctx"), None),
        P(("dp", "ctx"), None),
        P(("dp", "ctx"), None),
        P(("dp", "ctx"), None),
    )
    return jax.shard_map(
        on_device, mesh=mesh, in_specs=in_specs, out_specs=out_specs, check_vma=False
    )
```

```python
import jax
import jax.numpy as jnp
from jax import lax
from jax.experimental import pallas as pl
from jax.experimental.pallas import tpu as pltpu
from jax.sharding import PartitionSpec as P


HD = 64
NORM_EPS = 1e-05
SCORE_SCALE = 0.125
MASK_FILL = -1e30
SMALL = 12
PAD = 128
BOTH = ("dp", "ctx")


def layer_norm(values_in, gain, shift):
    center = values_in - jnp.mean(values_in, -1, keepdims=True)
    inv_std = lax.rsqrt(jnp.mean(center * center, -1, keepdims=True) + NORM_EPS)
    normed = center * inv_std
    return (normed * gain + shift, normed, inv_std)


def norm_back(upstream, gain, normed, inv_std):
    scaled = upstream * gain
    return inv_std * (
        scaled
        - jnp.mean(scaled, -1, keepdims=True)
        - normed * jnp.mean(scaled * normed, -1, keepdims=True)
    )


def gelu_back(pre_act, upstream):
    return jax.vjp(lambda values_in: jax.nn.gelu(values_in, approximate=True), pre_act)[1](
        upstream
    )[0]


def rows_product(left, right):
    return lax.dot_general(
        left, right, (((0,), (0,)), ((), ())), preferred_element_type=jnp.float32
    )


def times_transposed(left, right):
    return lax.dot_general(
        left, right, (((1,), (1,)), ((), ())), preferred_element_type=jnp.float32
    )


GRID = (4, 2, 2, 2)


def on_grid():
    return lax.axis_size("dp") == 16 and lax.axis_size("ctx") == 2


def place():
    at = lax.axis_index("dp")
    return at // 4, (at // 2) % 2, at % 2, lax.axis_index("ctx")


def move(block, axis, step):
    pairs = []
    for source in range(32):
        spot = [source // 8, (source // 4) % 2, (source // 2) % 2, source % 2]
        spot[axis] = (spot[axis] + step) % GRID[axis]
        pairs.append((source, ((spot[0] * 2 + spot[1]) * 2 + spot[2]) * 2 + spot[3]))
    return lax.ppermute(block, BOTH, pairs)


def joined(mine, theirs, at, axis):
    first = at == 0
    return jnp.stack([jnp.where(first, mine, theirs), jnp.where(first, theirs, mine)], axis)


def cut_of(columns):
    return columns // 256 * 128


def gather(shard):
    if not on_grid():
        return lax.all_gather(shard, BOTH, axis=0, tiled=False)
    z, y, c, x = place()
    held = [shard] + [move(shard, 0, step) for step in (1, 2, 3)]
    rows = []
    for spot in range(4):
        source = (z - spot) % 4
        row = held[0]
        for step in (1, 2, 3):
            row = jnp.where(source == step, held[step], row)
        rows.append(row)
    ring = jnp.stack(rows, 0)
    cut = cut_of(shard.shape[1])
    left, right = ring[..., :cut], ring[..., cut:]
    left = joined(left, move(left, 1, 1), y, 1)
    right = joined(right, move(right, 3, 1), x, 1)
    left = joined(left, move(left, 3, 1), x, 2)
    right = joined(right, move(right, 1, 1), y, 1)
    half = jnp.concatenate([left, right], -1)
    return joined(half, move(half, 2, 1), c, 2)


def taken(block, at, axis):
    return lax.dynamic_index_in_dim(block, at, axis, keepdims=False)


def added(block, at, axis, arrived):
    total = taken(block, at, axis).astype(jnp.float32) + arrived.astype(jnp.float32)
    return total.astype(jnp.bfloat16)


class Scatter:
    def __init__(self, grads, grid=True):
        devices = lax.axis_size("dp") * lax.axis_size("ctx")
        count, columns = grads.shape[0] // devices, grads.shape[1]
        self.grid = grid and on_grid()
        self.cut = cut_of(columns)
        self.held = grads.reshape((GRID if self.grid else (devices,)) + (count, columns))

    def core(self):
        if self.grid:
            c = place()[2]
            half = added(self.held, c, 2, move(taken(self.held, 1 - c, 2), 2, 1))
            self.held = (half[..., : self.cut], half[..., self.cut :])

    def first(self):
        if self.grid:
            _, y, _, x = place()
            left, right = self.held
            left = added(left, x, 2, move(taken(left, 1 - x, 2), 3, 1))
            right = added(right, y, 1, move(taken(right, 1 - y, 1), 1, 1))
            self.held = (left, right)

    def second(self):
        if self.grid:
            _, y, _, x = place()
            left, right = self.held
            left = added(left, y, 1, move(taken(left, 1 - y, 1), 1, 1))
            right = added(right, x, 1, move(taken(right, 1 - x, 1), 3, 1))
            self.held = jnp.concatenate([left, right], -1)

    def last(self):
        if not self.grid:
            return lax.psum_scatter(self.held, BOTH, scatter_dimension=0, tiled=False).astype(
                jnp.float32
            )
        z = place()[0]
        total = taken(self.held, z, 0).astype(jnp.float32)
        for step in (1, 2, 3):
            sent = taken(self.held, (z + step) % 4, 0)
            total = total + move(sent, 0, step).astype(jnp.float32)
        return total

    def all(self):
        self.core()
        self.first()
        self.second()
        return self.last()


def gate(value, *scatters):
    value, held = lax.optimization_barrier((value, [each.held for each in scatters]))
    for each, now in zip(scatters, held):
        each.held = now
    return value


LANES = 256


def one_head(block, head):
    lane = lax.broadcasted_iota(jnp.int32, block.shape, 1)
    return jnp.where(lane // HD == head, block, jnp.zeros_like(block))


def by_rows(left, right):
    return lax.dot_general(
        left, right, (((1,), (1,)), ((), ())), preferred_element_type=jnp.float32
    )


def own_scores(keys, queries):
    scores = by_rows(keys, queries)
    key_at = lax.broadcasted_iota(jnp.int32, scores.shape, 0)
    query_at = lax.broadcasted_iota(jnp.int32, scores.shape, 1)
    return jnp.where(key_at <= query_at, scores, MASK_FILL)


def far_scores(keys, queries, limit):
    key_at = lax.broadcasted_iota(jnp.int32, (keys.shape[0], 1), 0)
    return by_rows(keys, queries) + jnp.where(key_at < limit, 0.0, MASK_FILL)


def scaled(q):
    return (q.astype(jnp.float32) * SCORE_SCALE).astype(jnp.bfloat16)


def transposed(block):
    return block.astype(jnp.float32).T


def attend_kernel(limit, q_ref, ko_ref, vo_ref, kf_ref, vf_ref, out_ref, log_ref):
    own_values = transposed(vo_ref[0]).astype(jnp.bfloat16)
    far_values = transposed(vf_ref[0]).astype(jnp.bfloat16)
    parts = []
    small = scaled(q_ref[0])
    for head in range(LANES // HD):
        rows = slice(head * HD, (head + 1) * HD)
        queries = one_head(small, head)
        own = own_scores(ko_ref[0], queries)
        far = far_scores(kf_ref[0], queries, limit[0])
        peak = jnp.maximum(jnp.max(own, 0, keepdims=True), jnp.max(far, 0, keepdims=True))
        own = jnp.exp(own - peak)
        far = jnp.exp(far - peak)
        total = jnp.sum(own, 0, keepdims=True) + jnp.sum(far, 0, keepdims=True)
        log_ref[0, 0, head : head + 1, :] = peak + jnp.log(total)
        own = own.astype(jnp.bfloat16)
        far = far.astype(jnp.bfloat16)
        part = jnp.dot(own_values[rows], own, preferred_element_type=jnp.float32) + jnp.dot(
            far_values[rows], far, preferred_element_type=jnp.float32
        )
        parts.append(part * (1.0 / total))
    out_ref[0] = jnp.concatenate(parts, 0).T.astype(jnp.bfloat16)


def block_back(q, keys, values, d_att, attended, logs, scores_of):
    products = (d_att.astype(jnp.float32) * attended.astype(jnp.float32)).T
    keys_across = transposed(keys).astype(jnp.bfloat16)
    d_queries, d_keys, d_values = [], None, None
    small = scaled(q)
    for head in range(LANES // HD):
        rows = slice(head * HD, (head + 1) * HD)
        queries, d_head = one_head(small, head), one_head(d_att, head)
        delta = jnp.sum(products[rows], 0, keepdims=True)
        probs = jnp.exp(scores_of(keys, queries) - logs[head : head + 1])
        d_probs = by_rows(values, d_head)
        d_scores = (probs * (d_probs - delta)).astype(jnp.bfloat16)
        values_term = jnp.dot(
            probs.astype(jnp.bfloat16), d_head, preferred_element_type=jnp.float32
        )
        keys_term = jnp.dot(d_scores, queries, preferred_element_type=jnp.float32)
        d_values = values_term if head == 0 else d_values + values_term
        d_keys = keys_term if head == 0 else d_keys + keys_term
        d_queries.append(jnp.dot(keys_across[rows], d_scores, preferred_element_type=jnp.float32))
    return (jnp.concatenate(d_queries, 0) * SCORE_SCALE).T, d_keys, d_values


def far_kernel(limit, q_ref, k_ref, v_ref, d_ref, o_ref, log_ref, dq_ref, dkv_ref):
    d_queries, d_keys, d_values = block_back(
        q_ref[0], k_ref[0], v_ref[0], d_ref[0], o_ref[0], log_ref[0, 0],
        lambda keys, queries: far_scores(keys, queries, limit[0]),
    )
    dq_ref[0] = d_queries
    dkv_ref[0, 0] = d_keys.astype(jnp.bfloat16)
    dkv_ref[0, 1] = d_values.astype(jnp.bfloat16)


def own_kernel(
    q_ref, k_ref, v_ref, d_ref, o_ref, log_ref, before_ref, dq_ref, sum_ref, dkv_ref
):
    d_queries, d_keys, d_values = block_back(
        q_ref[0], k_ref[0], v_ref[0], d_ref[0], o_ref[0], log_ref[0, 0], own_scores
    )
    d_queries = d_queries + before_ref[0]
    dq_ref[0] = d_queries.astype(jnp.bfloat16)
    sum_ref[0] = jnp.sum(d_queries, 0, keepdims=True)
    dkv_ref[0, 0] = d_keys
    dkv_ref[0, 1] = d_values


def rows_spec(rows, skip=0, slot=0):
    return pl.BlockSpec((1, rows, LANES), lambda p, *_: (slot, 0, p + skip))


def log_spec(span):
    return pl.BlockSpec((1, 1, LANES // HD, span), lambda p, *_: (0, p, 0, 0))


def pair_spec(rows):
    return pl.BlockSpec((1, 2, rows, LANES), lambda p, *_: (0, 0, 0, p))


def attend(limit, queries, near, far, slot):
    _, span, width = queries.shape
    groups, reach = width // LANES, far.shape[1]
    return pl.pallas_call(
        attend_kernel,
        grid_spec=pltpu.PrefetchScalarGridSpec(
            num_scalar_prefetch=1,
            grid=(groups,),
            in_specs=[
                rows_spec(span, 0, slot),
                rows_spec(span, 0, slot),
                rows_spec(span, groups, slot),
                rows_spec(reach),
                rows_spec(reach, groups),
            ],
            out_specs=[rows_spec(span), log_spec(span)],
        ),
        out_shape=[
            jax.ShapeDtypeStruct((1, span, width), jnp.bfloat16),
            jax.ShapeDtypeStruct((1, groups, LANES // HD, span), jnp.float32),
        ],
        name="attend",
    )(limit, queries, near, near, far, far)


def far_back(limit, queries, far, d_att, attended, logs, slot):
    _, span, width = queries.shape
    groups, reach = width // LANES, far.shape[1]
    return pl.pallas_call(
        far_kernel,
        grid_spec=pltpu.PrefetchScalarGridSpec(
            num_scalar_prefetch=1,
            grid=(groups,),
            in_specs=[
                rows_spec(span, 0, slot),
                rows_spec(reach),
                rows_spec(reach, groups),
                rows_spec(span, 0, slot),
                rows_spec(span),
                log_spec(span),
            ],
            out_specs=[rows_spec(span), pair_spec(reach)],
        ),
        out_shape=[
            jax.ShapeDtypeStruct((1, span, width), jnp.float32),
            jax.ShapeDtypeStruct((1, 2, reach, width), jnp.bfloat16),
        ],
        name="far_back",
    )(limit, queries, far, far, d_att, attended, logs)


def own_back(queries, near, d_att, attended, logs, before, slot):
    _, span, width = queries.shape
    groups = width // LANES
    return pl.pallas_call(
        own_kernel,
        grid=(groups,),
        in_specs=[
            rows_spec(span, 0, slot),
            rows_spec(span, 0, slot),
            rows_spec(span, groups, slot),
            rows_spec(span, 0, slot),
            rows_spec(span),
            log_spec(span),
            rows_spec(span),
        ],
        out_specs=[
            rows_spec(span),
            pl.BlockSpec((1, 1, LANES), lambda p: (0, 0, p)),
            pair_spec(span),
        ],
        out_shape=[
            jax.ShapeDtypeStruct((1, span, width), jnp.bfloat16),
            jax.ShapeDtypeStruct((1, 1, width), jnp.float32),
            jax.ShapeDtypeStruct((1, 2, span, width), jnp.float32),
        ],
        name="own_back",
    )(queries, near, near, d_att, attended, logs, before)


def on_device(tokens_in, live_mask, cotangent, gains, biases, fc_bias, w_qkv, w_out, w_fc, w_proj):
    slot_count, span, width = tokens_in.shape
    row_count = slot_count * span
    devices = lax.axis_size("dp") * lax.axis_size("ctx")
    own_cols = width // devices
    units = fc_bias.shape[0] * devices
    per_col = units // width
    paired = lax.axis_size("ctx") == 2

    small = jnp.concatenate([gains.T, biases.T, fc_bias.reshape(own_cols, per_col)], 1)
    small = jnp.pad(small, ((0, 0), (0, PAD - SMALL)))
    first = gather(jnp.concatenate([w_qkv, small], 1)).reshape(width, 3 * width + PAD)
    rest = jnp.concatenate(
        [w_out] + [w_fc[:, i * width : (i + 1) * width] for i in range(per_col)] + [w_proj], 0
    )
    if on_grid():
        other = move(rest, 3, 1)
        rest = joined(rest, other, place()[3], 0)
        rest = lax.all_gather(rest, "dp", axis=0, tiled=True)
    else:
        rest = lax.all_gather(rest, BOTH, axis=0, tiled=False)
    qkv_weight = first[:, : 3 * width]
    small_all = first[:, 3 * width : 3 * width + SMALL].astype(jnp.float32)
    gain_rows = small_all[:, :2].T
    bias_rows = small_all[:, 2:8].T
    fc_shift = small_all[:, 8:].reshape(units)
    out_weight = rest[:, :own_cols].reshape(width, width)
    fc_weight = jnp.concatenate(
        [
            rest[:, (i + 1) * own_cols : (i + 2) * own_cols].reshape(width, width)
            for i in range(per_col)
        ],
        1,
    )
    proj_weight = rest[:, (1 + per_col) * own_cols :].reshape(units, width)

    keep_rows = jnp.repeat(live_mask.astype(jnp.float32), span)[:, None]
    hidden_in = tokens_in.reshape(row_count, width).astype(jnp.float32)
    ln_one, normed_one, inv_one = layer_norm(hidden_in, gain_rows[0], bias_rows[0])
    ln_one_b = ln_one.astype(jnp.bfloat16)
    projected = jnp.dot(ln_one_b, qkv_weight, preferred_element_type=jnp.float32)
    queries = (projected[:, :width] + bias_rows[1]).astype(jnp.bfloat16)
    keys_local = projected[:, width : 2 * width].astype(jnp.bfloat16)
    values_local = (projected[:, 2 * width :] + bias_rows[2]).astype(jnp.bfloat16)
    key_value = jnp.concatenate([keys_local, values_local], 1).reshape(slot_count, span, 2 * width)
    rank = lax.axis_index("ctx")
    limit = (rank * span).reshape(1).astype(jnp.int32)
    queries = queries.reshape(slot_count, span, width)
    before, attended_list, logs = [], [], []
    for slot in range(slot_count):
        block = key_value[slot : slot + 1]
        if paired:
            pairs = [(2 * i, 2 * i + 1) for i in range(devices // 2)]
            before.append(lax.ppermute(block, BOTH, pairs))
        else:
            before.append(lax.all_gather(block, "ctx", axis=1, tiled=True))
    for slot in range(slot_count):
        out, log = attend(limit, queries, key_value, before[slot], slot)
        attended_list.append(out)
        logs.append(log)
    attended = jnp.concatenate(attended_list, 0).reshape(row_count, width)
    after_attn = (
        hidden_in + jnp.dot(attended, out_weight, preferred_element_type=jnp.float32) + bias_rows[3]
    )
    ln_two, normed_two, inv_two = layer_norm(after_attn, gain_rows[1], bias_rows[4])
    ln_two_b = ln_two.astype(jnp.bfloat16)
    pre_act = jnp.dot(ln_two_b, fc_weight, preferred_element_type=jnp.float32) + fc_shift
    activated = jax.nn.gelu(pre_act, approximate=True).astype(jnp.bfloat16)
    final = (
        after_attn
        + jnp.dot(activated, proj_weight, preferred_element_type=jnp.float32)
        + bias_rows[5]
    )
    block_out = (keep_rows * final).astype(jnp.bfloat16).reshape(slot_count, span, width)

    upstream = keep_rows * cotangent.reshape(row_count, width).astype(jnp.float32)
    upstream_b = upstream.astype(jnp.bfloat16)
    sum_proj = Scatter(rows_product(activated, upstream_b).astype(jnp.bfloat16), False)
    out_proj = sum_proj.last()
    d_act = times_transposed(upstream_b, proj_weight)
    d_pre = gelu_back(pre_act, d_act)
    d_pre_b = d_pre.astype(jnp.bfloat16)
    sum_fc = Scatter(rows_product(ln_two_b, d_pre_b).astype(jnp.bfloat16))
    sum_fc.core()
    d_ln_two = times_transposed(d_pre_b, fc_weight)
    d_resid = upstream + norm_back(d_ln_two, gain_rows[1], normed_two, inv_two)
    d_resid_b = d_resid.astype(jnp.bfloat16)
    d_att = times_transposed(d_resid_b, out_weight).astype(jnp.bfloat16)
    d_att = gate(d_att, sum_fc).reshape(slot_count, span, width)
    sum_fc.first()
    d_far, arrived = [], []
    for slot in range(slot_count):
        d_part, terms = far_back(
            limit, queries, before[slot], d_att, attended_list[slot], logs[slot], slot
        )
        d_far.append(d_part)
        if paired:
            back = [(2 * i + 1, 2 * i) for i in range(devices // 2)]
            arrived.append(lax.ppermute(terms, BOTH, back))
        else:
            arrived.append(lax.psum_scatter(terms, "ctx", scatter_dimension=2, tiled=True))
    own_parts = []
    for slot in range(slot_count):
        own_parts.append(
            own_back(queries, key_value, d_att, attended_list[slot], logs[slot], d_far[slot], slot)
        )
    d_queries = jnp.concatenate([part[0] for part in own_parts], 0).reshape(row_count, width)
    query_sums = sum(part[1] for part in own_parts)
    d_queries = gate(d_queries, sum_fc)
    sum_fc.second()
    grad_query = rows_product(ln_one_b, d_queries).astype(jnp.bfloat16)
    grad_out = rows_product(attended, d_resid_b).astype(jnp.bfloat16)
    sum_mid = Scatter(jnp.concatenate([grad_query, grad_out], 1))
    sum_mid.core()
    arrived = gate(arrived, sum_fc, sum_mid)
    sum_mid.first()
    out_fc = sum_fc.last()
    own_terms = jnp.concatenate([part[2] for part in own_parts], 0) + jnp.concatenate(
        arrived, 0
    ).astype(jnp.float32)
    d_keys = own_terms[:, 0].reshape(row_count, width)
    d_values_own = own_terms[:, 1].reshape(row_count, width)
    d_proj_in = jnp.concatenate(
        [d_queries, d_keys.astype(jnp.bfloat16), d_values_own.astype(jnp.bfloat16)], 1
    )
    d_ln_one = times_transposed(d_proj_in, qkv_weight)
    sum_mid.second()
    grad_kv = rows_product(ln_one_b, d_proj_in[:, width:]).astype(jnp.bfloat16)
    d_input = d_resid + norm_back(d_ln_one, gain_rows[0], normed_one, inv_one)
    early = jnp.stack(
        [
            jnp.sum(d_ln_two * normed_two, 0),
            jnp.sum(query_sums, (0, 1)),
            jnp.sum(d_resid, 0),
            jnp.sum(d_ln_two, 0),
            jnp.sum(upstream, 0),
        ],
        0,
    )
    late = jnp.stack(
        [jnp.sum(d_ln_one * normed_one, 0), jnp.sum(d_ln_one, 0), jnp.sum(d_values_own, 0)], 0
    )
    grad_shift = jnp.sum(d_pre, 0).reshape(width, per_col).T
    grad_small = jnp.concatenate([early, grad_shift, late], 0).T.astype(jnp.bfloat16)
    grad_small = jnp.pad(grad_small, ((0, 0), (0, PAD - SMALL)))
    out_mid = sum_mid.last()
    last = Scatter(jnp.concatenate([grad_kv, grad_small], 1)).all()
    out_out = out_mid[:, width:]
    out_qkv = jnp.concatenate([out_mid[:, :width], last[:, : 2 * width]], 1)
    own = last[:, 2 * width : 2 * width + SMALL].T
    order = (10, 1, 11, 2, 3, 4)
    out_gain = jnp.stack([own[9], own[0]], 0)
    out_bias = jnp.stack([own[at] for at in order], 0)
    out_shift = own[5:9].T.reshape(own_cols * per_col)
    return (
        block_out,
        d_input.reshape(slot_count, span, width),
        out_gain,
        out_bias,
        out_shift,
        out_qkv,
        out_out,
        out_fc,
        out_proj,
    )


def solution(mesh):
    in_specs = (
        P("dp", "ctx", None),
        P("dp"),
        P("dp", "ctx", None),
        P(None, ("dp", "ctx")),
        P(None, ("dp", "ctx")),
        P(("dp", "ctx")),
        P(("dp", "ctx"), None),
        P(("dp", "ctx"), None),
        P(("dp", "ctx"), None),
        P(("dp", "ctx"), None),
    )
    out_specs = (
        P("dp", "ctx", None),
        P("dp", "ctx", None),
        P(None, ("dp", "ctx")),
        P(None, ("dp", "ctx")),
        P(("dp", "ctx")),
        P(("dp", "ctx"), None),
        P(("dp", "ctx"), None),
        P(("dp", "ctx"), None),
        P(("dp", "ctx"), None),
    )

    return jax.shard_map(
        on_device, mesh=mesh, in_specs=in_specs, out_specs=out_specs, check_vma=False
    )
```

```python
import jax
import jax.numpy as jnp
from jax import lax
from jax.experimental import pallas as pl
from jax.experimental.pallas import tpu as pltpu
from jax.sharding import PartitionSpec as P


HD = 64
NORM_EPS = 1e-05
SCORE_SCALE = 0.125
MASK_FILL = -1e30
SMALL = 12
PAD = 128
BOTH = ("dp", "ctx")


def layer_norm(values_in, gain, shift):
    center = values_in - jnp.mean(values_in, -1, keepdims=True)
    inv_std = lax.rsqrt(jnp.mean(center * center, -1, keepdims=True) + NORM_EPS)
    normed = center * inv_std
    return (normed * gain + shift, normed, inv_std)


def norm_back(upstream, gain, normed, inv_std):
    scaled = upstream * gain
    return inv_std * (
        scaled
        - jnp.mean(scaled, -1, keepdims=True)
        - normed * jnp.mean(scaled * normed, -1, keepdims=True)
    )


def gelu_back(pre_act, upstream):
    return jax.vjp(lambda values_in: jax.nn.gelu(values_in, approximate=True), pre_act)[1](
        upstream
    )[0]


def rows_product(left, right):
    return lax.dot_general(
        left, right, (((0,), (0,)), ((), ())), preferred_element_type=jnp.float32
    )


def times_transposed(left, right):
    return lax.dot_general(
        left, right, (((1,), (1,)), ((), ())), preferred_element_type=jnp.float32
    )


GRID = (4, 2, 2, 2)


def on_grid():
    return lax.axis_size("dp") == 16 and lax.axis_size("ctx") == 2


def place():
    at = lax.axis_index("dp")
    return at // 4, (at // 2) % 2, at % 2, lax.axis_index("ctx")


def move(block, axis, step):
    pairs = []
    for source in range(32):
        spot = [source // 8, (source // 4) % 2, (source // 2) % 2, source % 2]
        spot[axis] = (spot[axis] + step) % GRID[axis]
        pairs.append((source, ((spot[0] * 2 + spot[1]) * 2 + spot[2]) * 2 + spot[3]))
    return lax.ppermute(block, BOTH, pairs)


def joined(mine, theirs, at, axis):
    first = at == 0
    return jnp.stack([jnp.where(first, mine, theirs), jnp.where(first, theirs, mine)], axis)


def cut_of(columns):
    return columns // 256 * 128


def gather(shard):
    if not on_grid():
        return lax.all_gather(shard, BOTH, axis=0, tiled=False)
    z, y, c, x = place()
    held = [shard] + [move(shard, 0, step) for step in (1, 2, 3)]
    rows = []
    for spot in range(4):
        source = (z - spot) % 4
        row = held[0]
        for step in (1, 2, 3):
            row = jnp.where(source == step, held[step], row)
        rows.append(row)
    ring = jnp.stack(rows, 0)
    cut = cut_of(shard.shape[1])
    left, right = ring[..., :cut], ring[..., cut:]
    left = joined(left, move(left, 1, 1), y, 1)
    right = joined(right, move(right, 3, 1), x, 1)
    left = joined(left, move(left, 3, 1), x, 2)
    right = joined(right, move(right, 1, 1), y, 1)
    half = jnp.concatenate([left, right], -1)
    return joined(half, move(half, 2, 1), c, 2)


def taken(block, at, axis):
    return lax.dynamic_index_in_dim(block, at, axis, keepdims=False)


def summed(mine, arrived):
    return (mine.astype(jnp.float32) + arrived.astype(jnp.float32)).astype(jnp.bfloat16)


def added(block, at, axis, arrived):
    return summed(taken(block, at, axis), arrived)


class Scatter:
    def __init__(self, pieces, flat=False, y_first=True):
        devices = lax.axis_size("dp") * lax.axis_size("ctx")
        self.grid = on_grid() and not flat
        self.y_first = y_first
        lead = GRID if self.grid else (devices,)
        self.held = [
            piece.reshape(lead + (piece.shape[0] // devices, piece.shape[1])) for piece in pieces
        ]

    def core(self):
        if self.grid:
            c = place()[2]
            sent = jnp.concatenate([taken(piece, 1 - c, 2) for piece in self.held], -1)
            mine = jnp.concatenate([taken(piece, c, 2) for piece in self.held], -1)
            self.held = summed(mine, move(sent, 2, 1))

    def pair(self, axis, at, dim):
        self.held = added(self.held, at, dim, move(taken(self.held, 1 - at, dim), axis, 1))

    def first(self):
        if self.grid:
            _, y, _, x = place()
            self.pair(*((1, y, 1) if self.y_first else (3, x, 2)))

    def second(self):
        if self.grid:
            _, y, _, x = place()
            self.pair(*((3, x, 1) if self.y_first else (1, y, 1)))

    def last(self):
        if not self.grid:
            whole = jnp.concatenate(self.held, -1)
            return lax.psum_scatter(whole, BOTH, scatter_dimension=0, tiled=False).astype(
                jnp.float32
            )
        z = place()[0]
        total = taken(self.held, z, 0).astype(jnp.float32)
        for step in (1, 2, 3):
            sent = taken(self.held, (z + step) % 4, 0)
            total = total + move(sent, 0, step).astype(jnp.float32)
        return total


def gate(value, *scatters):
    value, held = lax.optimization_barrier((value, [each.held for each in scatters]))
    for each, now in zip(scatters, held):
        each.held = now
    return value


LANES = 256


def one_head(block, head):
    lane = lax.broadcasted_iota(jnp.int32, block.shape, 1)
    return jnp.where(lane // HD == head, block, jnp.zeros_like(block))


def by_rows(left, right):
    return lax.dot_general(
        left, right, (((1,), (1,)), ((), ())), preferred_element_type=jnp.float32
    )


def own_scores(keys, queries):
    scores = by_rows(keys, queries)
    key_at = lax.broadcasted_iota(jnp.int32, scores.shape, 0)
    query_at = lax.broadcasted_iota(jnp.int32, scores.shape, 1)
    return jnp.where(key_at <= query_at, scores, MASK_FILL)


def far_scores(keys, queries, limit):
    key_at = lax.broadcasted_iota(jnp.int32, (keys.shape[0], 1), 0)
    return by_rows(keys, queries) + jnp.where(key_at < limit, 0.0, MASK_FILL)


def scaled(q):
    return (q.astype(jnp.float32) * SCORE_SCALE).astype(jnp.bfloat16)


def transposed(block):
    return block.astype(jnp.float32).T


def attend_kernel(limit, q_ref, ko_ref, vo_ref, kf_ref, vf_ref, out_ref, log_ref):
    own_values = transposed(vo_ref[0]).astype(jnp.bfloat16)
    far_values = transposed(vf_ref[0]).astype(jnp.bfloat16)
    parts = []
    small = scaled(q_ref[0])
    for head in range(LANES // HD):
        rows = slice(head * HD, (head + 1) * HD)
        queries = one_head(small, head)
        own = own_scores(ko_ref[0], queries)
        far = far_scores(kf_ref[0], queries, limit[0])
        peak = jnp.maximum(jnp.max(own, 0, keepdims=True), jnp.max(far, 0, keepdims=True))
        own = jnp.exp(own - peak)
        far = jnp.exp(far - peak)
        total = jnp.sum(own, 0, keepdims=True) + jnp.sum(far, 0, keepdims=True)
        log_ref[0, 0, head : head + 1, :] = peak + jnp.log(total)
        own = own.astype(jnp.bfloat16)
        far = far.astype(jnp.bfloat16)
        part = jnp.dot(own_values[rows], own, preferred_element_type=jnp.float32) + jnp.dot(
            far_values[rows], far, preferred_element_type=jnp.float32
        )
        parts.append(part * (1.0 / total))
    out_ref[0] = jnp.concatenate(parts, 0).T.astype(jnp.bfloat16)


def block_back(q, keys, values, d_att, attended, logs, scores_of):
    products = (d_att.astype(jnp.float32) * attended.astype(jnp.float32)).T
    keys_across = transposed(keys).astype(jnp.bfloat16)
    d_queries, d_keys, d_values = [], None, None
    small = scaled(q)
    for head in range(LANES // HD):
        rows = slice(head * HD, (head + 1) * HD)
        queries, d_head = one_head(small, head), one_head(d_att, head)
        delta = jnp.sum(products[rows], 0, keepdims=True)
        probs = jnp.exp(scores_of(keys, queries) - logs[head : head + 1])
        d_probs = by_rows(values, d_head)
        d_scores = (probs * (d_probs - delta)).astype(jnp.bfloat16)
        values_term = jnp.dot(
            probs.astype(jnp.bfloat16), d_head, preferred_element_type=jnp.float32
        )
        keys_term = jnp.dot(d_scores, queries, preferred_element_type=jnp.float32)
        d_values = values_term if head == 0 else d_values + values_term
        d_keys = keys_term if head == 0 else d_keys + keys_term
        d_queries.append(jnp.dot(keys_across[rows], d_scores, preferred_element_type=jnp.float32))
    return (jnp.concatenate(d_queries, 0) * SCORE_SCALE).T, d_keys, d_values


def far_kernel(limit, q_ref, k_ref, v_ref, d_ref, o_ref, log_ref, dq_ref, dkv_ref):
    d_queries, d_keys, d_values = block_back(
        q_ref[0], k_ref[0], v_ref[0], d_ref[0], o_ref[0], log_ref[0, 0],
        lambda keys, queries: far_scores(keys, queries, limit[0]),
    )
    dq_ref[0] = d_queries
    dkv_ref[0, 0] = d_keys.astype(jnp.bfloat16)
    dkv_ref[0, 1] = d_values.astype(jnp.bfloat16)


def own_kernel(
    q_ref, k_ref, v_ref, d_ref, o_ref, log_ref, before_ref, dq_ref, sum_ref, dkv_ref
):
    d_queries, d_keys, d_values = block_back(
        q_ref[0], k_ref[0], v_ref[0], d_ref[0], o_ref[0], log_ref[0, 0], own_scores
    )
    d_queries = d_queries + before_ref[0]
    dq_ref[0] = d_queries.astype(jnp.bfloat16)
    sum_ref[0] = jnp.sum(d_queries, 0, keepdims=True)
    dkv_ref[0, 0] = d_keys
    dkv_ref[0, 1] = d_values


def rows_spec(rows, skip=0, slot=0):
    return pl.BlockSpec((1, rows, LANES), lambda p, *_: (slot, 0, p + skip))


def log_spec(span):
    return pl.BlockSpec((1, 1, LANES // HD, span), lambda p, *_: (0, p, 0, 0))


def pair_spec(rows):
    return pl.BlockSpec((1, 2, rows, LANES), lambda p, *_: (0, 0, 0, p))


def attend(limit, queries, near, far, slot):
    _, span, width = queries.shape
    groups, reach = width // LANES, far.shape[1]
    return pl.pallas_call(
        attend_kernel,
        grid_spec=pltpu.PrefetchScalarGridSpec(
            num_scalar_prefetch=1,
            grid=(groups,),
            in_specs=[
                rows_spec(span, 0, slot),
                rows_spec(span, 0, slot),
                rows_spec(span, groups, slot),
                rows_spec(reach),
                rows_spec(reach, groups),
            ],
            out_specs=[rows_spec(span), log_spec(span)],
        ),
        out_shape=[
            jax.ShapeDtypeStruct((1, span, width), jnp.bfloat16),
            jax.ShapeDtypeStruct((1, groups, LANES // HD, span), jnp.float32),
        ],
        name="attend",
    )(limit, queries, near, near, far, far)


def far_back(limit, queries, far, d_att, attended, logs, slot):
    _, span, width = queries.shape
    groups, reach = width // LANES, far.shape[1]
    return pl.pallas_call(
        far_kernel,
        grid_spec=pltpu.PrefetchScalarGridSpec(
            num_scalar_prefetch=1,
            grid=(groups,),
            in_specs=[
                rows_spec(span, 0, slot),
                rows_spec(reach),
                rows_spec(reach, groups),
                rows_spec(span, 0, slot),
                rows_spec(span),
                log_spec(span),
            ],
            out_specs=[rows_spec(span), pair_spec(reach)],
        ),
        out_shape=[
            jax.ShapeDtypeStruct((1, span, width), jnp.float32),
            jax.ShapeDtypeStruct((1, 2, reach, width), jnp.bfloat16),
        ],
        name="far_back",
    )(limit, queries, far, far, d_att, attended, logs)


def own_back(queries, near, d_att, attended, logs, before, slot):
    _, span, width = queries.shape
    groups = width // LANES
    return pl.pallas_call(
        own_kernel,
        grid=(groups,),
        in_specs=[
            rows_spec(span, 0, slot),
            rows_spec(span, 0, slot),
            rows_spec(span, groups, slot),
            rows_spec(span, 0, slot),
            rows_spec(span),
            log_spec(span),
            rows_spec(span),
        ],
        out_specs=[
            rows_spec(span),
            pl.BlockSpec((1, 1, LANES), lambda p: (0, 0, p)),
            pair_spec(span),
        ],
        out_shape=[
            jax.ShapeDtypeStruct((1, span, width), jnp.bfloat16),
            jax.ShapeDtypeStruct((1, 1, width), jnp.float32),
            jax.ShapeDtypeStruct((1, 2, span, width), jnp.float32),
        ],
        name="own_back",
    )(queries, near, near, d_att, attended, logs, before)


def on_device(tokens_in, live_mask, cotangent, gains, biases, fc_bias, w_qkv, w_out, w_fc, w_proj):
    slot_count, span, width = tokens_in.shape
    row_count = slot_count * span
    devices = lax.axis_size("dp") * lax.axis_size("ctx")
    own_cols = width // devices
    units = fc_bias.shape[0] * devices
    per_col = units // width
    paired = lax.axis_size("ctx") == 2

    small = jnp.concatenate([gains.T, biases.T, fc_bias.reshape(own_cols, per_col)], 1)
    small = jnp.pad(small, ((0, 0), (0, PAD - SMALL)))
    first = gather(jnp.concatenate([w_qkv, small], 1)).reshape(width, 3 * width + PAD)
    rest = jnp.concatenate(
        [w_out] + [w_fc[:, i * width : (i + 1) * width] for i in range(per_col)] + [w_proj], 0
    )
    if on_grid():
        other = move(rest, 3, 1)
        rest = joined(rest, other, place()[3], 0)
        rest = lax.all_gather(rest, "dp", axis=0, tiled=True)
    else:
        rest = lax.all_gather(rest, BOTH, axis=0, tiled=False)
    qkv_weight = first[:, : 3 * width]
    small_all = first[:, 3 * width : 3 * width + SMALL].astype(jnp.float32)
    gain_rows = small_all[:, :2].T
    bias_rows = small_all[:, 2:8].T
    fc_shift = small_all[:, 8:].reshape(units)
    out_weight = rest[:, :own_cols].reshape(width, width)
    fc_weight = jnp.concatenate(
        [
            rest[:, (i + 1) * own_cols : (i + 2) * own_cols].reshape(width, width)
            for i in range(per_col)
        ],
        1,
    )
    proj_weight = rest[:, (1 + per_col) * own_cols :].reshape(units, width)

    keep_rows = jnp.repeat(live_mask.astype(jnp.float32), span)[:, None]
    hidden_in = tokens_in.reshape(row_count, width).astype(jnp.float32)
    ln_one, normed_one, inv_one = layer_norm(hidden_in, gain_rows[0], bias_rows[0])
    ln_one_b = ln_one.astype(jnp.bfloat16)
    projected = jnp.dot(ln_one_b, qkv_weight, preferred_element_type=jnp.float32)
    queries = (projected[:, :width] + bias_rows[1]).astype(jnp.bfloat16)
    keys_local = projected[:, width : 2 * width].astype(jnp.bfloat16)
    values_local = (projected[:, 2 * width :] + bias_rows[2]).astype(jnp.bfloat16)
    key_value = jnp.concatenate([keys_local, values_local], 1).reshape(slot_count, span, 2 * width)
    rank = lax.axis_index("ctx")
    limit = (rank * span).reshape(1).astype(jnp.int32)
    queries = queries.reshape(slot_count, span, width)
    before, attended_list, logs = [], [], []
    for slot in range(slot_count):
        block = key_value[slot : slot + 1]
        if paired:
            pairs = [(2 * i, 2 * i + 1) for i in range(devices // 2)]
            before.append(lax.ppermute(block, BOTH, pairs))
        else:
            before.append(lax.all_gather(block, "ctx", axis=1, tiled=True))
    upstream = keep_rows * cotangent.reshape(row_count, width).astype(jnp.float32)
    upstream_b = upstream.astype(jnp.bfloat16)
    waited = (before[0], key_value, queries, fc_shift, upstream_b, bias_rows, jnp.sum(upstream, 0))
    waited = lax.optimization_barrier(waited)
    before[0], key_value, queries, fc_shift, upstream_b, bias_rows, upstream_sum = waited
    for slot in range(slot_count):
        out, log = attend(limit, queries, key_value, before[slot], slot)
        attended_list.append(out)
        logs.append(log)
    attended = jnp.concatenate(attended_list, 0).reshape(row_count, width)
    after_attn = (
        hidden_in + jnp.dot(attended, out_weight, preferred_element_type=jnp.float32) + bias_rows[3]
    )
    ln_two, normed_two, inv_two = layer_norm(after_attn, gain_rows[1], bias_rows[4])
    ln_two_b = ln_two.astype(jnp.bfloat16)
    pre_act = jnp.dot(ln_two_b, fc_weight, preferred_element_type=jnp.float32) + fc_shift
    activated = jax.nn.gelu(pre_act, approximate=True).astype(jnp.bfloat16)
    final = (
        after_attn
        + jnp.dot(activated, proj_weight, preferred_element_type=jnp.float32)
        + bias_rows[5]
    )

    sum_proj = Scatter([rows_product(activated, upstream_b).astype(jnp.bfloat16)], True)
    out_proj = sum_proj.last()
    d_act = times_transposed(upstream_b, proj_weight)
    d_pre = gelu_back(pre_act, d_act)
    d_pre_b = d_pre.astype(jnp.bfloat16)
    sum_fc = Scatter([rows_product(ln_two_b, d_pre_b).astype(jnp.bfloat16)])
    sum_fc.core()
    d_ln_two = times_transposed(d_pre_b, fc_weight)
    d_resid = upstream + norm_back(d_ln_two, gain_rows[1], normed_two, inv_two)
    d_resid_b = d_resid.astype(jnp.bfloat16)
    d_att = times_transposed(d_resid_b, out_weight).astype(jnp.bfloat16)
    d_att = gate(d_att, sum_fc).reshape(slot_count, span, width)
    sum_fc.first()
    d_far, arrived = [], []
    for slot in range(slot_count):
        d_part, terms = far_back(
            limit, queries, before[slot], d_att, attended_list[slot], logs[slot], slot
        )
        d_far.append(d_part)
        if paired:
            back = [(2 * i + 1, 2 * i) for i in range(devices // 2)]
            arrived.append(lax.ppermute(terms, BOTH, back))
        else:
            arrived.append(lax.psum_scatter(terms, "ctx", scatter_dimension=2, tiled=True))
    own_parts = []
    for slot in range(slot_count):
        own_parts.append(
            own_back(queries, key_value, d_att, attended_list[slot], logs[slot], d_far[slot], slot)
        )
    d_queries = jnp.concatenate([part[0] for part in own_parts], 0).reshape(row_count, width)
    query_sums = sum(part[1] for part in own_parts)
    grad_query = rows_product(ln_one_b, d_queries).astype(jnp.bfloat16)
    grad_out = rows_product(attended, d_resid_b).astype(jnp.bfloat16)
    sum_mid = Scatter([grad_query, grad_out], False, False)
    sum_mid.core()
    arrived, final = gate((arrived, final), sum_fc, sum_mid)
    block_out = (keep_rows * final).astype(jnp.bfloat16).reshape(slot_count, span, width)
    sum_fc.second()
    sum_mid.first()
    own_terms = jnp.concatenate([part[2] for part in own_parts], 0) + jnp.concatenate(
        arrived, 0
    ).astype(jnp.float32)
    d_keys = own_terms[:, 0].reshape(row_count, width)
    d_values_own = own_terms[:, 1].reshape(row_count, width)
    d_proj_in = jnp.concatenate(
        [d_queries, d_keys.astype(jnp.bfloat16), d_values_own.astype(jnp.bfloat16)], 1
    )
    d_ln_one = times_transposed(d_proj_in, qkv_weight)
    grad_kv = rows_product(ln_one_b, d_proj_in[:, width:]).astype(jnp.bfloat16)
    d_input = d_resid + norm_back(d_ln_one, gain_rows[0], normed_one, inv_one)
    early = jnp.stack(
        [
            jnp.sum(d_ln_two * normed_two, 0),
            jnp.sum(query_sums, (0, 1)),
            jnp.sum(d_resid, 0),
            jnp.sum(d_ln_two, 0),
            upstream_sum,
        ],
        0,
    )
    late = jnp.stack(
        [jnp.sum(d_ln_one * normed_one, 0), jnp.sum(d_ln_one, 0), jnp.sum(d_values_own, 0)], 0
    )
    grad_shift = jnp.sum(d_pre, 0).reshape(width, per_col).T
    grad_small = jnp.concatenate([early, grad_shift, late], 0).T.astype(jnp.bfloat16)
    grad_small = jnp.pad(grad_small, ((0, 0), (0, PAD - SMALL)))
    sum_last = Scatter([grad_kv, grad_small])
    sum_last.core()
    out_fc = sum_fc.last()
    sum_mid.second()
    sum_last.first()
    out_mid = sum_mid.last()
    sum_last.second()
    last = sum_last.last()
    out_out = out_mid[:, width:]
    out_qkv = jnp.concatenate([out_mid[:, :width], last[:, : 2 * width]], 1)
    own = last[:, 2 * width : 2 * width + SMALL].T
    order = (10, 1, 11, 2, 3, 4)
    out_gain = jnp.stack([own[9], own[0]], 0)
    out_bias = jnp.stack([own[at] for at in order], 0)
    out_shift = own[5:9].T.reshape(own_cols * per_col)
    return (
        block_out,
        d_input.reshape(slot_count, span, width),
        out_gain,
        out_bias,
        out_shift,
        out_qkv,
        out_out,
        out_fc,
        out_proj,
    )


def solution(mesh):
    in_specs = (
        P("dp", "ctx", None),
        P("dp"),
        P("dp", "ctx", None),
        P(None, ("dp", "ctx")),
        P(None, ("dp", "ctx")),
        P(("dp", "ctx")),
        P(("dp", "ctx"), None),
        P(("dp", "ctx"), None),
        P(("dp", "ctx"), None),
        P(("dp", "ctx"), None),
    )
    out_specs = (
        P("dp", "ctx", None),
        P("dp", "ctx", None),
        P(None, ("dp", "ctx")),
        P(None, ("dp", "ctx")),
        P(("dp", "ctx")),
        P(("dp", "ctx"), None),
        P(("dp", "ctx"), None),
        P(("dp", "ctx"), None),
        P(("dp", "ctx"), None),
    )

    return jax.shard_map(
        on_device, mesh=mesh, in_specs=in_specs, out_specs=out_specs, check_vma=False
    )
```

```python
import jax
import jax.numpy as jnp
from jax import lax
from jax.experimental import pallas as pl
from jax.experimental.pallas import tpu as pltpu
from jax.sharding import PartitionSpec as P


HD = 64
NORM_EPS = 1e-05
SCORE_SCALE = 0.125
MASK_FILL = -1e30
SMALL = 12
PAD = 128
BOTH = ("dp", "ctx")


def layer_norm(values_in, gain, shift):
    center = values_in - jnp.mean(values_in, -1, keepdims=True)
    inv_std = lax.rsqrt(jnp.mean(center * center, -1, keepdims=True) + NORM_EPS)
    normed = center * inv_std
    return (normed * gain + shift, normed, inv_std)


def norm_back(upstream, gain, normed, inv_std):
    scaled = upstream * gain
    return inv_std * (
        scaled
        - jnp.mean(scaled, -1, keepdims=True)
        - normed * jnp.mean(scaled * normed, -1, keepdims=True)
    )


def gelu_back(pre_act, upstream):
    return jax.vjp(lambda values_in: jax.nn.gelu(values_in, approximate=True), pre_act)[1](
        upstream
    )[0]


def rows_product(left, right):
    return lax.dot_general(
        left, right, (((0,), (0,)), ((), ())), preferred_element_type=jnp.float32
    )


def times_transposed(left, right):
    return lax.dot_general(
        left, right, (((1,), (1,)), ((), ())), preferred_element_type=jnp.float32
    )


GRID = (4, 2, 2, 2)


def on_grid():
    return lax.axis_size("dp") == 16 and lax.axis_size("ctx") == 2


def place():
    at = lax.axis_index("dp")
    return at // 4, (at // 2) % 2, at % 2, lax.axis_index("ctx")


def move(block, axis, step):
    pairs = []
    for source in range(32):
        spot = [source // 8, (source // 4) % 2, (source // 2) % 2, source % 2]
        spot[axis] = (spot[axis] + step) % GRID[axis]
        pairs.append((source, ((spot[0] * 2 + spot[1]) * 2 + spot[2]) * 2 + spot[3]))
    return lax.ppermute(block, BOTH, pairs)


def joined(mine, theirs, at, axis):
    first = at == 0
    return jnp.stack([jnp.where(first, mine, theirs), jnp.where(first, theirs, mine)], axis)


def cut_of(columns):
    return columns // 256 * 128


def gather(shard):
    if not on_grid():
        return lax.all_gather(shard, BOTH, axis=0, tiled=False)
    z, y, c, x = place()
    held = [shard] + [move(shard, 0, step) for step in (1, 2, 3)]
    rows = []
    for spot in range(4):
        source = (z - spot) % 4
        row = held[0]
        for step in (1, 2, 3):
            row = jnp.where(source == step, held[step], row)
        rows.append(row)
    ring = jnp.stack(rows, 0)
    cut = cut_of(shard.shape[1])
    left, right = ring[..., :cut], ring[..., cut:]
    left = joined(left, move(left, 1, 1), y, 1)
    right = joined(right, move(right, 3, 1), x, 1)
    left = joined(left, move(left, 3, 1), x, 2)
    right = joined(right, move(right, 1, 1), y, 1)
    half = jnp.concatenate([left, right], -1)
    return joined(half, move(half, 2, 1), c, 2)


def taken(block, at, axis):
    return lax.dynamic_index_in_dim(block, at, axis, keepdims=False)


def summed(mine, arrived):
    return mine.astype(jnp.float32) + arrived.astype(jnp.float32)


class Scatter:
    def __init__(self, pieces, flat=False):
        devices = lax.axis_size("dp") * lax.axis_size("ctx")
        self.grid = on_grid() and not flat
        self.left = ["z", "y", "x"]
        lead = GRID if self.grid else (devices,)
        self.held = [
            piece.reshape(lead + (piece.shape[0] // devices, piece.shape[1])) for piece in pieces
        ]

    def core(self):
        if self.grid:
            c = place()[2]
            sent = jnp.concatenate([taken(piece, 1 - c, 2) for piece in self.held], -1)
            mine = jnp.concatenate([taken(piece, c, 2) for piece in self.held], -1)
            self.held = summed(mine, move(sent, 2, 1)).astype(jnp.bfloat16)

    def stage(self, name):
        if not self.grid:
            return
        z, y, _, x = place()
        axis, at, size = {"z": (0, z, 4), "y": (1, y, 2), "x": (3, x, 2)}[name]
        dim = self.left.index(name)
        self.left.remove(name)
        total = taken(self.held, at, dim)
        for step in range(1, size):
            total = summed(total, move(taken(self.held, (at + step) % size, dim), axis, step))
        self.held = total.astype(jnp.bfloat16) if self.left else total

    def halves(self):
        cut = self.held.shape[-1] // 256 * 128 if self.grid else 0
        parts = []
        for part in (slice(0, cut), slice(cut, None)):
            half = Scatter([])
            half.grid, half.left = self.grid, list(self.left)
            half.held = self.held[..., part] if self.grid else None
            parts.append(half)
        return parts

    def join(self, parts):
        if self.grid:
            self.left = list(parts[0].left)
            self.held = jnp.concatenate([part.held for part in parts], -1)

    def result(self):
        if self.grid:
            return self.held
        whole = jnp.concatenate(self.held, -1)
        return lax.psum_scatter(whole, BOTH, scatter_dimension=0, tiled=False).astype(jnp.float32)


def gate(value, *scatters):
    value, held = lax.optimization_barrier((value, [each.held for each in scatters]))
    for each, now in zip(scatters, held):
        each.held = now
    return value


LANES = 256


def one_head(block, head):
    lane = lax.broadcasted_iota(jnp.int32, block.shape, 1)
    return jnp.where(lane // HD == head, block, jnp.zeros_like(block))


def by_rows(left, right):
    return lax.dot_general(
        left, right, (((1,), (1,)), ((), ())), preferred_element_type=jnp.float32
    )


def own_scores(keys, queries):
    scores = by_rows(keys, queries)
    key_at = lax.broadcasted_iota(jnp.int32, scores.shape, 0)
    query_at = lax.broadcasted_iota(jnp.int32, scores.shape, 1)
    return jnp.where(key_at <= query_at, scores, MASK_FILL)


def far_scores(keys, queries, limit):
    key_at = lax.broadcasted_iota(jnp.int32, (keys.shape[0], 1), 0)
    return by_rows(keys, queries) + jnp.where(key_at < limit, 0.0, MASK_FILL)


def scaled(q):
    return (q.astype(jnp.float32) * SCORE_SCALE).astype(jnp.bfloat16)


def transposed(block):
    return block.astype(jnp.float32).T


def attend_kernel(limit, q_ref, ko_ref, vo_ref, kf_ref, vf_ref, out_ref, log_ref):
    own_values = transposed(vo_ref[0]).astype(jnp.bfloat16)
    far_values = transposed(vf_ref[0]).astype(jnp.bfloat16)
    parts = []
    small = scaled(q_ref[0])
    for head in range(LANES // HD):
        rows = slice(head * HD, (head + 1) * HD)
        queries = one_head(small, head)
        own = own_scores(ko_ref[0], queries)
        far = far_scores(kf_ref[0], queries, limit[0])
        peak = jnp.maximum(jnp.max(own, 0, keepdims=True), jnp.max(far, 0, keepdims=True))
        own = jnp.exp(own - peak)
        far = jnp.exp(far - peak)
        total = jnp.sum(own, 0, keepdims=True) + jnp.sum(far, 0, keepdims=True)
        log_ref[0, 0, head : head + 1, :] = peak + jnp.log(total)
        own = own.astype(jnp.bfloat16)
        far = far.astype(jnp.bfloat16)
        part = jnp.dot(own_values[rows], own, preferred_element_type=jnp.float32) + jnp.dot(
            far_values[rows], far, preferred_element_type=jnp.float32
        )
        parts.append(part * (1.0 / total))
    out_ref[0] = jnp.concatenate(parts, 0).T.astype(jnp.bfloat16)


def block_back(q, keys, values, d_att, attended, logs, scores_of):
    products = (d_att.astype(jnp.float32) * attended.astype(jnp.float32)).T
    keys_across = transposed(keys).astype(jnp.bfloat16)
    d_queries, d_keys, d_values = [], None, None
    small = scaled(q)
    for head in range(LANES // HD):
        rows = slice(head * HD, (head + 1) * HD)
        queries, d_head = one_head(small, head), one_head(d_att, head)
        delta = jnp.sum(products[rows], 0, keepdims=True)
        probs = jnp.exp(scores_of(keys, queries) - logs[head : head + 1])
        d_probs = by_rows(values, d_head)
        d_scores = (probs * (d_probs - delta)).astype(jnp.bfloat16)
        values_term = jnp.dot(
            probs.astype(jnp.bfloat16), d_head, preferred_element_type=jnp.float32
        )
        keys_term = jnp.dot(d_scores, queries, preferred_element_type=jnp.float32)
        d_values = values_term if head == 0 else d_values + values_term
        d_keys = keys_term if head == 0 else d_keys + keys_term
        d_queries.append(jnp.dot(keys_across[rows], d_scores, preferred_element_type=jnp.float32))
    return (jnp.concatenate(d_queries, 0) * SCORE_SCALE).T, d_keys, d_values


def far_kernel(limit, q_ref, k_ref, v_ref, d_ref, o_ref, log_ref, dq_ref, dkv_ref):
    d_queries, d_keys, d_values = block_back(
        q_ref[0], k_ref[0], v_ref[0], d_ref[0], o_ref[0], log_ref[0, 0],
        lambda keys, queries: far_scores(keys, queries, limit[0]),
    )
    dq_ref[0] = d_queries
    dkv_ref[0, 0] = d_keys.astype(jnp.bfloat16)
    dkv_ref[0, 1] = d_values.astype(jnp.bfloat16)


def own_kernel(
    q_ref, k_ref, v_ref, d_ref, o_ref, log_ref, before_ref, dq_ref, sum_ref, dkv_ref
):
    d_queries, d_keys, d_values = block_back(
        q_ref[0], k_ref[0], v_ref[0], d_ref[0], o_ref[0], log_ref[0, 0], own_scores
    )
    d_queries = d_queries + before_ref[0]
    dq_ref[0] = d_queries.astype(jnp.bfloat16)
    sum_ref[0] = jnp.sum(d_queries, 0, keepdims=True)
    dkv_ref[0, 0] = d_keys
    dkv_ref[0, 1] = d_values


def rows_spec(rows, skip=0, slot=0):
    return pl.BlockSpec((1, rows, LANES), lambda p, *_: (slot, 0, p + skip))


def log_spec(span):
    return pl.BlockSpec((1, 1, LANES // HD, span), lambda p, *_: (0, p, 0, 0))


def pair_spec(rows):
    return pl.BlockSpec((1, 2, rows, LANES), lambda p, *_: (0, 0, 0, p))


def attend(limit, queries, near, far, slot):
    _, span, width = queries.shape
    groups, reach = width // LANES, far.shape[1]
    return pl.pallas_call(
        attend_kernel,
        grid_spec=pltpu.PrefetchScalarGridSpec(
            num_scalar_prefetch=1,
            grid=(groups,),
            in_specs=[
                rows_spec(span, 0, slot),
                rows_spec(span, 0, slot),
                rows_spec(span, groups, slot),
                rows_spec(reach),
                rows_spec(reach, groups),
            ],
            out_specs=[rows_spec(span), log_spec(span)],
        ),
        out_shape=[
            jax.ShapeDtypeStruct((1, span, width), jnp.bfloat16),
            jax.ShapeDtypeStruct((1, groups, LANES // HD, span), jnp.float32),
        ],
        name="attend",
    )(limit, queries, near, near, far, far)


def far_back(limit, queries, far, d_att, attended, logs, slot):
    _, span, width = queries.shape
    groups, reach = width // LANES, far.shape[1]
    return pl.pallas_call(
        far_kernel,
        grid_spec=pltpu.PrefetchScalarGridSpec(
            num_scalar_prefetch=1,
            grid=(groups,),
            in_specs=[
                rows_spec(span, 0, slot),
                rows_spec(reach),
                rows_spec(reach, groups),
                rows_spec(span, 0, slot),
                rows_spec(span),
                log_spec(span),
            ],
            out_specs=[rows_spec(span), pair_spec(reach)],
        ),
        out_shape=[
            jax.ShapeDtypeStruct((1, span, width), jnp.float32),
            jax.ShapeDtypeStruct((1, 2, reach, width), jnp.bfloat16),
        ],
        name="far_back",
    )(limit, queries, far, far, d_att, attended, logs)


def own_back(queries, near, d_att, attended, logs, before, slot):
    _, span, width = queries.shape
    groups = width // LANES
    return pl.pallas_call(
        own_kernel,
        grid=(groups,),
        in_specs=[
            rows_spec(span, 0, slot),
            rows_spec(span, 0, slot),
            rows_spec(span, groups, slot),
            rows_spec(span, 0, slot),
            rows_spec(span),
            log_spec(span),
            rows_spec(span),
        ],
        out_specs=[
            rows_spec(span),
            pl.BlockSpec((1, 1, LANES), lambda p: (0, 0, p)),
            pair_spec(span),
        ],
        out_shape=[
            jax.ShapeDtypeStruct((1, span, width), jnp.bfloat16),
            jax.ShapeDtypeStruct((1, 1, width), jnp.float32),
            jax.ShapeDtypeStruct((1, 2, span, width), jnp.float32),
        ],
        name="own_back",
    )(queries, near, near, d_att, attended, logs, before)


def on_device(tokens_in, live_mask, cotangent, gains, biases, fc_bias, w_qkv, w_out, w_fc, w_proj):
    slot_count, span, width = tokens_in.shape
    row_count = slot_count * span
    devices = lax.axis_size("dp") * lax.axis_size("ctx")
    own_cols = width // devices
    units = fc_bias.shape[0] * devices
    per_col = units // width
    paired = lax.axis_size("ctx") == 2

    small = jnp.concatenate([gains.T, biases.T, fc_bias.reshape(own_cols, per_col)], 1)
    small = jnp.pad(small, ((0, 0), (0, PAD - SMALL)))
    first = gather(jnp.concatenate([w_qkv, small], 1)).reshape(width, 3 * width + PAD)
    rest = jnp.concatenate(
        [w_out] + [w_fc[:, i * width : (i + 1) * width] for i in range(per_col)] + [w_proj], 0
    )
    if on_grid():
        other = move(rest, 3, 1)
        rest = joined(rest, other, place()[3], 0)
        rest = lax.all_gather(rest, "dp", axis=0, tiled=True)
    else:
        rest = lax.all_gather(rest, BOTH, axis=0, tiled=False)
    qkv_weight = first[:, : 3 * width]
    small_all = first[:, 3 * width : 3 * width + SMALL].astype(jnp.float32)
    gain_rows = small_all[:, :2].T
    bias_rows = small_all[:, 2:8].T
    fc_shift = small_all[:, 8:].reshape(units)
    out_weight = rest[:, :own_cols].reshape(width, width)
    fc_weight = jnp.concatenate(
        [
            rest[:, (i + 1) * own_cols : (i + 2) * own_cols].reshape(width, width)
            for i in range(per_col)
        ],
        1,
    )
    proj_weight = rest[:, (1 + per_col) * own_cols :].reshape(units, width)

    keep_rows = jnp.repeat(live_mask.astype(jnp.float32), span)[:, None]
    hidden_in = tokens_in.reshape(row_count, width).astype(jnp.float32)
    ln_one, normed_one, inv_one = layer_norm(hidden_in, gain_rows[0], bias_rows[0])
    ln_one_b = ln_one.astype(jnp.bfloat16)
    projected = jnp.dot(ln_one_b, qkv_weight, preferred_element_type=jnp.float32)
    queries = (projected[:, :width] + bias_rows[1]).astype(jnp.bfloat16)
    keys_local = projected[:, width : 2 * width].astype(jnp.bfloat16)
    values_local = (projected[:, 2 * width :] + bias_rows[2]).astype(jnp.bfloat16)
    key_value = jnp.concatenate([keys_local, values_local], 1)
    key_value = key_value.reshape(slot_count, span, 2 * width)
    rank = lax.axis_index("ctx")
    limit = (rank * span).reshape(1).astype(jnp.int32)
    queries = queries.reshape(slot_count, span, width)
    before, attended_list, logs = [], [], []
    for slot in range(slot_count):
        rows = slice(slot * span, (slot + 1) * span)
        block = jnp.concatenate([keys_local[rows], values_local[rows]], 1)[None]
        if paired:
            pairs = [(2 * i, 2 * i + 1) for i in range(devices // 2)]
            before.append(lax.ppermute(block, BOTH, pairs))
        else:
            before.append(lax.all_gather(block, "ctx", axis=1, tiled=True))
    upstream = keep_rows * cotangent.reshape(row_count, width).astype(jnp.float32)
    upstream_b = upstream.astype(jnp.bfloat16)
    upstream_sum = jnp.sum(upstream, 0)
    waited = (before[0], key_value, queries, fc_shift, upstream_b, bias_rows, upstream_sum)
    waited = lax.optimization_barrier(waited)
    before[0], key_value, queries, fc_shift, upstream_b, bias_rows, upstream_sum = waited
    for slot in range(slot_count):
        out, log = attend(limit, queries, key_value, before[slot], slot)
        attended_list.append(out)
        logs.append(log)
    attended = jnp.concatenate(attended_list, 0).reshape(row_count, width)
    after_attn = (
        hidden_in + jnp.dot(attended, out_weight, preferred_element_type=jnp.float32) + bias_rows[3]
    )
    ln_two, normed_two, inv_two = layer_norm(after_attn, gain_rows[1], bias_rows[4])
    ln_two_b = ln_two.astype(jnp.bfloat16)
    pre_act = jnp.dot(ln_two_b, fc_weight, preferred_element_type=jnp.float32) + fc_shift
    activated = jax.nn.gelu(pre_act, approximate=True).astype(jnp.bfloat16)
    final = (
        after_attn
        + jnp.dot(activated, proj_weight, preferred_element_type=jnp.float32)
        + bias_rows[5]
    )

    sum_proj = Scatter([rows_product(activated, upstream_b).astype(jnp.bfloat16)], True)
    out_proj = sum_proj.result()
    d_act = times_transposed(upstream_b, proj_weight)
    d_pre = gelu_back(pre_act, d_act)
    d_pre_b = d_pre.astype(jnp.bfloat16)
    sum_fc = Scatter([rows_product(ln_two_b, d_pre_b).astype(jnp.bfloat16)])
    sum_fc.core()
    d_ln_two = times_transposed(d_pre_b, fc_weight)
    d_resid = upstream + norm_back(d_ln_two, gain_rows[1], normed_two, inv_two)
    d_resid_b = d_resid.astype(jnp.bfloat16)
    d_att = times_transposed(d_resid_b, out_weight).astype(jnp.bfloat16)
    d_att = gate(d_att, sum_fc).reshape(slot_count, span, width)
    sum_fc.stage("y")
    d_far, arrived = [], []
    for slot in range(slot_count):
        d_part, terms = far_back(
            limit, queries, before[slot], d_att, attended_list[slot], logs[slot], slot
        )
        d_far.append(d_part)
        if paired:
            back = [(2 * i + 1, 2 * i) for i in range(devices // 2)]
            arrived.append(lax.ppermute(terms, BOTH, back))
        else:
            arrived.append(lax.psum_scatter(terms, "ctx", scatter_dimension=2, tiled=True))
    own_parts = []
    for slot in range(slot_count):
        own_parts.append(
            own_back(queries, key_value, d_att, attended_list[slot], logs[slot], d_far[slot], slot)
        )
    d_queries = jnp.concatenate([part[0] for part in own_parts], 0).reshape(row_count, width)
    query_sums = sum(part[1] for part in own_parts)
    grad_query = rows_product(ln_one_b, d_queries).astype(jnp.bfloat16)
    grad_out = rows_product(attended, d_resid_b).astype(jnp.bfloat16)
    sum_mid = Scatter([grad_query, grad_out])
    sum_mid.core()
    arrived, final = gate((arrived, final), sum_fc, sum_mid)
    sum_mid.stage("y")
    sum_fc.stage("z")
    block_out = (keep_rows * final).astype(jnp.bfloat16).reshape(slot_count, span, width)
    own_terms = jnp.concatenate([part[2] for part in own_parts], 0) + jnp.concatenate(
        arrived, 0
    ).astype(jnp.float32)
    sum_mid.stage("x")
    sum_fc.stage("x")
    d_keys = own_terms[:, 0].reshape(row_count, width)
    d_values_own = own_terms[:, 1].reshape(row_count, width)
    d_proj_in = jnp.concatenate(
        [d_queries, d_keys.astype(jnp.bfloat16), d_values_own.astype(jnp.bfloat16)], 1
    )
    d_ln_one = times_transposed(d_proj_in, qkv_weight)
    grad_kv = rows_product(ln_one_b, d_proj_in[:, width:]).astype(jnp.bfloat16)
    d_input = d_resid + norm_back(d_ln_one, gain_rows[0], normed_one, inv_one)
    early = jnp.stack(
        [
            jnp.sum(d_ln_two * normed_two, 0),
            jnp.sum(query_sums, (0, 1)),
            jnp.sum(d_resid, 0),
            jnp.sum(d_ln_two, 0),
            upstream_sum,
        ],
        0,
    )
    late = jnp.stack(
        [jnp.sum(d_ln_one * normed_one, 0), jnp.sum(d_ln_one, 0), jnp.sum(d_values_own, 0)], 0
    )
    grad_shift = jnp.sum(d_pre, 0).reshape(width, per_col).T
    grad_small = jnp.concatenate([early, grad_shift, late], 0).T.astype(jnp.bfloat16)
    grad_small = jnp.pad(grad_small, ((0, 0), (0, PAD - SMALL)))
    sum_last = Scatter([grad_kv, grad_small])
    sum_last.core()
    sum_mid.stage("z")
    parts = sum_last.halves()
    parts[0].stage("x")
    parts[1].stage("y")
    parts[0].stage("y")
    parts[1].stage("x")
    sum_last.join(parts)
    sum_last.stage("z")
    out_fc, out_mid, last = sum_fc.result(), sum_mid.result(), sum_last.result()
    out_out = out_mid[:, width:]
    out_qkv = jnp.concatenate([out_mid[:, :width], last[:, : 2 * width]], 1)
    own = last[:, 2 * width : 2 * width + SMALL].T
    order = (10, 1, 11, 2, 3, 4)
    out_gain = jnp.stack([own[9], own[0]], 0)
    out_bias = jnp.stack([own[at] for at in order], 0)
    out_shift = own[5:9].T.reshape(own_cols * per_col)
    return (
        block_out,
        d_input.reshape(slot_count, span, width),
        out_gain,
        out_bias,
        out_shift,
        out_qkv,
        out_out,
        out_fc,
        out_proj,
    )


def solution(mesh):
    in_specs = (
        P("dp", "ctx", None),
        P("dp"),
        P("dp", "ctx", None),
        P(None, ("dp", "ctx")),
        P(None, ("dp", "ctx")),
        P(("dp", "ctx")),
        P(("dp", "ctx"), None),
        P(("dp", "ctx"), None),
        P(("dp", "ctx"), None),
        P(("dp", "ctx"), None),
    )
    out_specs = (
        P("dp", "ctx", None),
        P("dp", "ctx", None),
        P(None, ("dp", "ctx")),
        P(None, ("dp", "ctx")),
        P(("dp", "ctx")),
        P(("dp", "ctx"), None),
        P(("dp", "ctx"), None),
        P(("dp", "ctx"), None),
        P(("dp", "ctx"), None),
    )

    return jax.shard_map(
        on_device, mesh=mesh, in_specs=in_specs, out_specs=out_specs, check_vma=False
    )
```
